256 devices in a mesh: row: 16 (over y, z_lo), col: 16 (over z_hi, x, core).
Axes of the slice: x: 4, y: 4, z: 8 (z_hi: 2, z_lo: 4; z = z_hi * 4 + z_lo), core: 2. Of those that a mesh axis runs over, the one named last changes fastest.
Arguments:
- laplacian: float32 [23040, 23040], P('row', 'col'), may hold values from -1 to 1.12, as said below
- block: float32 [23040, 256], P(('row', 'col')), may hold values from -6 to 6
- bounds: float32 [2], replicated, may hold values from 0.25 to 2.1, as said below
Outputs:
- filtered: float32 [23040, 256], P(('row', 'col'))
- rayleigh: float32 [256, 256], replicated
The draws below stay inside these ranges and needn't reach their ends.
Inputs may be any that keep to these rules, and one draw needn't show every extreme that they name: laplacian is symmetric; its diagonal entries lie in 0.88 to 1.12 and its other entries have magnitude at most 1.14 / sqrt(23040). bounds[0] lies in 0.25 to 0.40 and bounds[1] in 1.95 to 2.10.
All inputs are finite; a program needn't handle non-finite values.
Results may differ from the reference program's by a relative error of at most 0.00025.
Values sent between devices are 32-bit elements; how exact they have to be, the bound alone decides.
A program may use at most 64 MiB of HBM per device.

```python
import math
import jax
import jax.numpy as jnp
from jax import lax

K = 256
N = 23040


def draw_laplacian(key, part):
    first_key, second_key = jax.random.split(key)
    spread = 1.04 / math.sqrt(N)
    diagonal_spread = 0.05
    entries = jax.random.uniform(first_key, (N, N), jnp.float32, -spread, spread)
    symmetric = (entries + entries.T) * 0.5
    diagonal = 1.0 + jax.random.uniform(second_key, (N,), jnp.float32, -diagonal_spread, diagonal_spread)
    positions = jnp.arange(N)
    return symmetric.at[positions, positions].set(diagonal)


def draw_bounds(key, part):
    values = jax.random.uniform(key, (2,), jnp.float32, 0.0, 1.0)
    return jnp.stack([0.25 + 0.15 * values[0], 1.95 + 0.15 * values[1]])


def steps_of(own_key, extent, cuts, low, largest):
    gain, own = 1.0, jax.random.fold_in(own_key, 6)
    for dim, shards_of in cuts:
        heights = jnp.exp(jax.random.uniform(jax.random.fold_in(own, dim), (shards_of,), jnp.float32, low / len(cuts), largest / len(cuts)))
        gain = gain * jnp.repeat(heights, extent[dim] // shards_of).reshape([-1 if axis == dim else 1 for axis in range(len(extent))])
    return gain


def centred(own_key, dims, scale, limit, cuts=(), dtype=jnp.bfloat16):
    drawn = scale * jax.random.normal(own_key, dims, jnp.float32)
    if cuts:
        drawn = drawn * steps_of(own_key, dims, cuts, -0.22, 0.18)
    return jnp.clip(drawn, -limit, limit).astype(dtype)


def setup_inputs(seed: int = 0) -> dict:
    seeds = jax.random.split(jax.random.key(seed), 4)
    return {
        "laplacian": draw_laplacian(jax.random.fold_in(seeds[3], 71), 0),
        "block": centred(seeds[1], (N, K), 1.0, 6.0, ((0, 256),), jnp.float32),
        "bounds": draw_bounds(jax.random.fold_in(seeds[3], 71), 0),
    }


def reference(laplacian, block, bounds):
    lower_bound = bounds[0]
    upper_bound = bounds[1]
    center = (upper_bound + lower_bound) * 0.5
    half_width = (upper_bound - lower_bound) * 0.5

    def shifted_product(vectors):
        return jnp.dot(laplacian.astype(jnp.float32), vectors.astype(jnp.float32), precision=lax.Precision.HIGHEST, preferred_element_type=jnp.float32) - center * vectors
    previous = block
    current = shifted_product(block) / half_width
    for degree_step in range(3):
        following = 2.0 / half_width * shifted_product(current) - previous
        previous = current
        current = following
    filtered = current
    image_full = shifted_product(filtered)
    gram = jnp.dot(filtered.T.astype(jnp.float32), filtered.astype(jnp.float32), precision=lax.Precision.HIGHEST, preferred_element_type=jnp.float32)
    projected = jnp.dot(filtered.T.astype(jnp.float32), image_full.astype(jnp.float32), precision=lax.Precision.HIGHEST, preferred_element_type=jnp.float32) + center * gram
    projected = (projected + projected.T) * 0.5
    factor = jnp.linalg.cholesky(gram)
    first_solve = jax.scipy.linalg.solve_triangular(factor, projected, lower=True)
    rayleigh = jax.scipy.linalg.solve_triangular(factor, first_solve.T, lower=True)
    return (filtered, rayleigh)
```

```python
import functools

import jax
import jax.numpy as jnp
from jax import lax
from jax.experimental import pallas as pl
from jax.experimental.pallas import tpu as pltpu
from jax.sharding import PartitionSpec as P

MESH = pl.DeviceIdType.MESH
F32 = jnp.float32
BF16 = jnp.bfloat16
L = 128
TILE = 1440
PAD = 1536
PIECE = 96
OWN = 90
LEAD = 0

CHAIN = dict(
    raw0=((2, 4, 2, PIECE, L), F32),
    panel0=((PAD, L), F32),
    panel_r=((2, 4, 2, PIECE, L), F32),
    panel_c=((4, 4, 2, 48, L), F32),
    panel_f=((4, 4, 2, 48, L), F32),
    part_c=((4, 4, 2, 48, L), F32),
    part_r=((2, 4, 2, PIECE, L), F32),
    vcat=((PAD, 2 * L), BF16),
    core_in=((4, 2, PIECE, L), F32),
    y_in=((6, 2, 2, 48, L), F32),
    y_sum=((4, 2, 48, L), F32),
    z_in=((6, 48, L), F32),
    x_in=((6, PIECE, L), F32),
    x_sum=((2, PIECE, L), F32),
    h_in=((PIECE, L), F32),
    z1=((2, 48, L), F32),
    z2=((PIECE, L), F32),
    z4=((2, 48, L), F32),
)
REDUCE = dict(
    a=((2, 4, 4, 8, 256), F32),
    total=((2, 4, 4, 8, 256), F32),
    core_in=((4, 4, 8, 256), F32),
    x_in=((3, 4, 8, 256), F32),
    y_in=((3, 8, 256), F32),
    z_in=((4, 8, 256), F32),
    h_own=((8, 256), F32),
    h_in=((8, 256), F32),
)
SHARED = dict(
    stage=((TILE, TILE), F32),
    strip=((128, PAD), F32),
    mat_h=((PAD, PAD), BF16),
    mat_l=((PAD, PAD), BF16),
    tra_h=((PAD, PAD), BF16),
    tra_l=((PAD, PAD), BF16),
    own4=((128, 256), F32),
    ft_h=((256, PAD), BF16),
    ft_l=((256, PAD), BF16),
    img_h=((PAD, 256), BF16),
    img_l=((PAD, 256), BF16),
)
AT_START, AT_ROW, AT_ROWG, AT_COL, AT_COLG, AT_TURN, AT_LAST, CHAIN_SEMS = 0, 11, 23, 33, 42, 53, 54, 64
REDUCE_SEMS = 18


def split(value):
    high = value.astype(BF16)
    return high, (value - high.astype(F32)).astype(BF16)


def run(tasks):
    tasks = list(tasks)
    while tasks:
        tasks = [t for t in tasks if next(t, "end") != "end"]


class Kernel:
    def __init__(self):
        r, c = lax.axis_index("row"), lax.axis_index("col")
        self.r, self.c = r, c
        self.y, self.z = r // 4, r % 4
        self.zh, self.x, self.core = c // 8, (c // 2) % 4, c % 2
        self.pos = self.core * 8 + self.x * 2 + self.zh

    def yn(self, d):
        return ((self.y + d) % 4) * 4 + self.z, self.c

    def zn(self, d):
        return self.y * 4 + (self.z + d) % 4, self.c

    def xn(self, d):
        return self.r, self.zh * 8 + ((self.x + d) % 4) * 2 + self.core

    def hn(self):
        return self.r, (1 - self.zh) * 8 + self.x * 2 + self.core

    def cn(self):
        return self.r, self.zh * 8 + self.x * 2 + 1 - self.core

    def turn_to(self):
        return self.pos, self.r

    def turn_from(self):
        r = self.r
        return self.c, (r % 2) * 8 + ((r // 2) % 4) * 2 + r // 8


class Link:
    def __init__(self, send, recv):
        self.send, self.recv, self.open = send, recv, []

    def put(self, src, dst, k, device):
        copy = pltpu.make_async_remote_copy(
            src_ref=src, dst_ref=dst, send_sem=self.send.at[k], recv_sem=self.recv.at[k], device_id=device, device_id_type=MESH
        )
        copy.start()
        self.open.append(copy)

    def got(self, dst, k, device):
        pltpu.make_async_remote_copy(
            src_ref=dst, dst_ref=dst, send_sem=self.send.at[k], recv_sem=self.recv.at[k], device_id=device, device_id_type=MESH
        ).wait_recv()

    def flush(self):
        for copy in self.open:
            copy.wait_send()
        self.open = []


def ring_sum(link, k, i, near, half, box, out, ready):
    a, b, d = (i + 1) % 4, (i + 3) % 4, (i + 2) % 4
    ready(d)
    link.put(half(d, 0), box.at[0], k, near(1))
    link.put(half(d, 1), box.at[1], k + 1, near(3))
    ready(a)
    link.put(half(a, 1), box.at[2], k + 2, near(1))
    ready(b)
    link.put(half(b, 0), box.at[3], k + 3, near(3))
    ready(i)
    yield
    link.got(box.at[0], k, near(3))
    half(a, 0)[...] += box[0]
    link.put(half(a, 0), box.at[4], k + 4, near(1))
    link.got(box.at[1], k + 1, near(1))
    half(b, 1)[...] += box[1]
    link.put(half(b, 1), box.at[5], k + 5, near(3))
    yield
    link.got(box.at[2], k + 2, near(3))
    link.got(box.at[3], k + 3, near(1))
    link.got(box.at[4], k + 4, near(3))
    link.got(box.at[5], k + 5, near(1))
    out(0, half(i, 0)[...] + box[4] + box[3])
    out(1, half(i, 1)[...] + box[2] + box[5])


def nothing(j):
    pass


def gather_col(me, link, k, panel):
    core, x, zh = me.core, me.x, me.zh
    a, b, d = (x + 1) % 4, (x + 3) % 4, (x + 2) % 4

    def put(ref, j, device):
        link.put(ref, ref, k + j, device)

    put(panel.at[core, x, zh], 0, me.hn())
    put(panel.at[core, x, zh], 1, me.xn(1))
    put(panel.at[core, x, zh], 2, me.xn(3))
    yield
    link.got(panel.at[core, x, 1 - zh], k, me.hn())
    put(panel.at[core, x, 1 - zh], 3, me.xn(1))
    put(panel.at[core, x, 1 - zh], 4, me.xn(3))
    put(panel.at[core, x], 7, me.cn())
    yield
    link.got(panel.at[core, b, zh], k + 1, me.xn(3))
    link.got(panel.at[core, b, 1 - zh], k + 3, me.xn(3))
    put(panel.at[core, b, 0], 5, me.xn(1))
    put(panel.at[core, b], 8, me.cn())
    link.got(panel.at[core, a, zh], k + 2, me.xn(1))
    link.got(panel.at[core, a, 1 - zh], k + 4, me.xn(1))
    put(panel.at[core, a, 1], 6, me.xn(3))
    put(panel.at[core, a], 9, me.cn())
    yield
    link.got(panel.at[core, d, 0], k + 5, me.xn(3))
    link.got(panel.at[core, d, 1], k + 6, me.xn(1))
    put(panel.at[core, d], 10, me.cn())
    yield
    other = 1 - core
    link.got(panel.at[other, x], k + 7, me.cn())
    link.got(panel.at[other, b], k + 8, me.cn())
    link.got(panel.at[other, a], k + 9, me.cn())
    link.got(panel.at[other, d], k + 10, me.cn())


def gather_row(me, link, k, panel):
    y, z = me.y, me.z
    za, zb, zd = (z + 1) % 4, (z + 3) % 4, (z + 2) % 4
    ya, yb, yd = (y + 1) % 4, (y + 3) % 4, (y + 2) % 4

    def put(ref, j, device):
        link.put(ref, ref, k + j, device)

    put(panel.at[y, z], 0, me.zn(1))
    put(panel.at[y, z], 1, me.zn(3))
    yield
    link.got(panel.at[y, zb], k, me.zn(3))
    put(panel.at[y, zb, 0], 2, me.zn(1))
    link.got(panel.at[y, za], k + 1, me.zn(1))
    put(panel.at[y, za, 1], 3, me.zn(3))
    yield
    link.got(panel.at[y, zd, 0], k + 2, me.zn(3))
    link.got(panel.at[y, zd, 1], k + 3, me.zn(1))
    low, high = pl.ds(0, 2), pl.ds(2, 2)
    put(panel.at[y, low], 4, me.yn(1))
    put(panel.at[y, high], 5, me.yn(3))
    put(panel.at[y, high], 6, me.yn(1))
    put(panel.at[y, low], 7, me.yn(3))
    yield
    link.got(panel.at[yb, low], k + 4, me.yn(3))
    put(panel.at[yb, low], 8, me.yn(1))
    link.got(panel.at[ya, high], k + 5, me.yn(1))
    put(panel.at[ya, high], 9, me.yn(3))
    yield
    link.got(panel.at[yb, high], k + 6, me.yn(3))
    link.got(panel.at[ya, low], k + 7, me.yn(1))
    link.got(panel.at[yd, low], k + 8, me.yn(3))
    link.got(panel.at[yd, high], k + 9, me.yn(1))


def split_row_panel(panel, vcat):
    @pl.loop(0, 8)
    def _(i):
        high, low = split(panel[i // 4, i % 4].reshape(2 * PIECE, L))
        rows = pl.ds(pl.multiple_of(i * 192, 192), 192)
        vcat[rows, :L] = high
        vcat[rows, L:] = low


def split_col_panel(panel, vcat):
    @pl.loop(0, 4)
    def _(i):
        high, low = split(panel[i].reshape(384, L))
        rows = pl.ds(pl.multiple_of(i * 384, 384), 384)
        vcat[rows, :L] = high
        vcat[rows, L:] = low


def product(high, low, vcat, chunk):
    rows = pl.ds(pl.multiple_of(chunk * 384, 384), 384)
    wide = jnp.dot(high[rows, :], vcat[...], preferred_element_type=F32)
    rest = jnp.dot(low[rows, :], vcat[:, :L], preferred_element_type=F32)
    return wide[:, :L] + (wide[:, L:] + rest)


def odd_step(me, link, s, b, scale, previous, save):
    split_row_panel(b["panel_r"], b["vcat"]) if previous is not None else None
    part, y_sum, panel = b["part_c"], b["y_sum"], b["panel_c"]
    y, z = me.y, me.z

    def ready(j):
        part[j] = product(s["tra_h"], s["tra_l"], b["vcat"], j).reshape(4, 2, 48, L)

    def out_y(h, value):
        y_sum[pl.ds(2 * h, 2)] = value

    def out_z(h, value):
        value = value * scale
        if previous is not None:
            value = value - previous[h]
        panel[y, z, h] = value
        if save is not None:
            save[h] = value

    yield from ring_sum(link, AT_ROW, y, me.yn, lambda j, h: part.at[j, pl.ds(2 * h, 2)], b["y_in"], out_y, ready)
    yield from ring_sum(link, AT_ROW + 6, z, me.zn, lambda j, h: y_sum.at[j, h], b["z_in"], out_z, nothing)
    yield from gather_row(me, link, AT_ROWG, panel)
    link.flush()


def even_sum(me, link, s, b, scale, previous, store):
    split_col_panel(b["panel_c"], b["vcat"])
    part, box = b["part_r"], b["core_in"]
    core, x, zh = me.core, me.x, me.zh
    other, first = 1 - core, 1 - x // 2
    k = AT_COL

    def compute(half, pair):
        value = product(s["mat_h"], s["mat_l"], b["vcat"], half * 2 + pair)
        part[half, pl.ds(2 * pair, 2)] = value.reshape(2, 2, PIECE, L)

    compute(other, first)
    link.put(part.at[other, pl.ds(2 * first, 2)], box.at[pl.ds(2 * first, 2)], k, me.cn())
    last = 1 - first
    compute(other, last)
    link.put(part.at[other, pl.ds(2 * last, 2)], box.at[pl.ds(2 * last, 2)], k + 1, me.cn())
    compute(core, first)
    compute(core, last)
    yield
    turn = []

    def ready(j):
        if len(turn) == 0:
            link.got(box.at[pl.ds(2 * first, 2)], k, me.cn())
        if len(turn) == 1:
            link.got(box.at[pl.ds(2 * last, 2)], k + 1, me.cn())
        turn.append(j)
        part[core, j] += box[j]

    x_sum = b["x_sum"]

    def out_x(h, value):
        x_sum[h] = value

    yield from ring_sum(link, k + 2, x, me.xn, lambda j, h: part.at[core, j, h], b["x_in"], out_x, ready)
    link.put(x_sum.at[1 - zh], b["h_in"], k + 8, me.hn())
    yield
    link.got(b["h_in"], k + 8, me.hn())
    store((x_sum[zh] + b["h_in"][...]) * scale - previous())


def chain(me, link, s, b, half_width, first):
    def scaled(n):
        return n / half_width

    yield from gather_col(me, link, AT_START, b["raw0"])
    panel0 = b["panel0"]
    panel0[TILE:, :] = jnp.zeros((PAD - TILE, L), F32)
    for c in range(16):
        panel0[c * OWN : (c + 1) * OWN, :] = b["raw0"][c % 2, (c // 2) % 4, c // 8, :OWN, :]

    @pl.loop(0, 4)
    def _(i):
        rows = pl.ds(pl.multiple_of(i * 384, 384), 384)
        high, low = split(panel0[rows, :])
        b["vcat"][rows, :L] = high
        b["vcat"][rows, L:] = low

    if first is not None:
        first()
    link.flush()
    yield from odd_step(me, link, s, b, scaled(1.0), None, b["z1"])
    z2, panel_r = b["z2"], b["panel_r"]

    def store2(value):
        z2[...] = value
        panel_r[me.core, me.x, me.zh] = value

    rows = pl.ds(pl.multiple_of(me.pos * PIECE, PIECE), PIECE)
    yield from even_sum(me, link, s, b, scaled(2.0), lambda: panel0[rows, :], store2)
    yield from gather_col(me, link, AT_COLG, panel_r)
    link.flush()
    yield from odd_step(me, link, s, b, scaled(2.0), b["z1"], None)

    def store4(value):
        panel_r[me.core, me.x, me.zh] = value
        b["z4"][...] = value.reshape(2, 48, L)

    yield from even_sum(me, link, s, b, scaled(2.0), lambda: z2[...], store4)
    link.flush()


def turned_gather(me, link, b, alone):
    panel, z4 = b["panel_f"], b["z4"]
    row, col = me.turn_to()
    slot = panel.at[row // 4, row % 4]

    def copy():
        return pltpu.make_async_remote_copy(
            src_ref=z4,
            dst_ref=slot,
            send_sem=link.send.at[AT_TURN],
            recv_sem=link.recv.at[AT_TURN],
            device_id=(row, col),
            device_id_type=MESH,
        )

    @pl.when(jnp.logical_not(alone))
    def _():
        copy().start()

    @pl.when(alone)
    def _():
        panel[me.y, me.z] = z4[...]

    yield

    @pl.when(jnp.logical_not(alone))
    def _():
        link.got(panel.at[me.y, me.z], AT_TURN, me.turn_from())
        copy().wait_send()

    yield from gather_row(me, link, AT_LAST, panel)


def all_sum(me, link, b):
    a, total = b["a"], b["total"]
    y, z, zh, x, core = me.y, me.z, me.zh, me.x, me.core
    other = 1 - core
    link.put(a.at[other], b["core_in"], 0, me.cn())
    yield
    link.got(b["core_in"], 0, me.cn())
    a[core] += b["core_in"][...]
    for d in (1, 2, 3):
        link.put(a.at[core, (x + d) % 4], b["x_in"].at[d - 1], d, me.xn(d))
    yield
    for d in (1, 2, 3):
        link.got(b["x_in"].at[d - 1], d, me.xn(4 - d))
    a[core, x] += (b["x_in"][0] + b["x_in"][1]) + b["x_in"][2]
    for d in (1, 2, 3):
        link.put(a.at[core, x, (y + d) % 4], b["y_in"].at[d - 1], 3 + d, me.yn(d))
    yield
    for d in (1, 2, 3):
        link.got(b["y_in"].at[d - 1], 3 + d, me.yn(4 - d))
    own = a[core, x, y] + ((b["y_in"][0] + b["y_in"][1]) + b["y_in"][2])
    b["z_in"][z] = own
    for d in (1, 2, 3):
        link.put(b["z_in"].at[z], b["z_in"].at[z], 6 + d, me.zn(d))
    yield
    for d in (1, 2, 3):
        link.got(b["z_in"].at[(z + 4 - d) % 4], 6 + d, me.zn(4 - d))
    b["h_own"][...] = (b["z_in"][0] + b["z_in"][1]) + (b["z_in"][2] + b["z_in"][3])
    link.put(b["h_own"], b["h_in"], 10, me.hn())
    yield
    link.got(b["h_in"], 10, me.hn())
    link.flush()
    total[core, x, y] = b["h_own"][...] + b["h_in"][...]
    for d in (1, 2, 3):
        link.put(total.at[core, x, y], total.at[core, x, y], 10 + d, me.yn(d))
    yield
    for d in (1, 2, 3):
        link.got(total.at[core, x, (y + 4 - d) % 4], 10 + d, me.yn(4 - d))
    for d in (1, 2, 3):
        link.put(total.at[core, x], total.at[core, x], 13 + d, me.xn(d))
    yield
    for d in (1, 2, 3):
        link.got(total.at[core, (x + 4 - d) % 4], 13 + d, me.xn(4 - d))
    link.put(total.at[core], total.at[core], 17, me.cn())
    yield
    link.got(total.at[other], 17, me.cn())
    link.flush()


def body_kernel(lap, block, bounds, filtered, gram, projected, *scratch):
    names = list(SHARED), list(CHAIN), list(CHAIN), list(REDUCE), list(REDUCE)
    groups, at = [], 0
    for group in names:
        groups.append(dict(zip(group, scratch[at : at + len(group)])))
        at += len(group)
    s, *chains, red_g, red_p = groups
    lap_sem, *sems = scratch[at:]
    links = [Link(sems[2 * i], sems[2 * i + 1]) for i in range(4)]
    me = Kernel()
    to_row, to_col = me.turn_to()
    alone = jnp.logical_and(to_row == me.r, to_col == me.c)

    load = pltpu.make_async_copy(lap, s["stage"], lap_sem)
    load.start()
    for h, b in enumerate(chains):
        own = b["raw0"].at[me.core, me.x, me.zh]
        own[OWN - 2 :, :] = jnp.zeros((PIECE - OWN + 2, L), F32)
        own[:OWN, :] = block[:, h * L : (h + 1) * L]

    barrier = pltpu.get_barrier_semaphore()
    near = [f(d) for f in (me.yn, me.zn, me.xn) for d in (1, 2, 3)] + [me.hn(), me.cn()]
    for device in near:
        pl.semaphore_signal(barrier, inc=1, device_id=device, device_id_type=MESH)

    @pl.when(jnp.logical_not(alone))
    def _():
        pl.semaphore_signal(barrier, inc=1, device_id=me.turn_to(), device_id_type=MESH)
        pl.semaphore_signal(barrier, inc=1, device_id=me.turn_from(), device_id_type=MESH)

    pl.semaphore_wait(barrier, jnp.where(alone, len(near), len(near) + 2))

    center = (bounds[1] + bounds[0]) * 0.5
    half_width = (bounds[1] - bounds[0]) * 0.5

    def prepare():
        load.wait()
        shift = jnp.where(me.r == me.c, center, 0.0)
        strip = s["strip"]
        strip[...] = jnp.zeros_like(strip)

        def strip_of(start, count):
            value = s["stage"][pl.ds(start, count), :]
            row = start + lax.broadcasted_iota(jnp.int32, (count, TILE), 0)
            col = lax.broadcasted_iota(jnp.int32, (count, TILE), 1)
            strip[:count, :TILE] = value - jnp.where(row == col, shift, 0.0)

        def spread(start):
            whole = strip[...]
            high, low = split(whole)
            s["mat_h"][pl.ds(start, 128), :] = high
            s["mat_l"][pl.ds(start, 128), :] = low
            high, low = split(whole.T)
            s["tra_h"][:, pl.ds(start, 128)] = high
            s["tra_l"][:, pl.ds(start, 128)] = low

        @pl.loop(0, TILE // 128)
        def _(i):
            start = pl.multiple_of(i * 128, 128)
            strip_of(start, 128)
            spread(start)

        strip[...] = jnp.zeros_like(strip)
        strip_of(TILE // 128 * 128, TILE % 128)
        spread(TILE // 128 * 128)

    one = chain(me, links[0], s, chains[0], half_width, prepare)
    two = chain(me, links[1], s, chains[1], half_width, None)
    next(one)
    next(two)
    for _ in range(LEAD):
        next(one)
    run([one, two])

    own4 = s["own4"]
    own4[PIECE:, :] = jnp.zeros((128 - PIECE, 256), F32)
    for h, b in enumerate(chains):
        own4[:PIECE, h * L : (h + 1) * L] = b["z4"][...].reshape(PIECE, L)
    high, low = split(own4[...])
    dims = (((0,), (0,)), ((), ()))

    def pair(p, q):
        return lax.dot_general(p, q, dims, preferred_element_type=F32)

    part = pair(high, high) + (pair(high, low) + pair(low, high))
    red_g["a"][...] = part.reshape(2, 4, 4, 8, 256)
    run(
        [gather_col(me, links[h], AT_COLG, chains[h]["panel_r"]) for h in (0, 1)]
        + [turned_gather(me, links[h], chains[h], alone) for h in (0, 1)]
        + [all_sum(me, links[2], red_g)]
    )
    for link in links[:2]:
        link.flush()
    for c in range(16):

        @pl.when(me.c == c)
        def _(c=c):
            for h, b in enumerate(chains):
                row = 0
                while row < OWN:
                    at = c * OWN + row
                    p, inside = at // PIECE, at % PIECE
                    count = min(PIECE - inside, OWN - row)
                    filtered[row : row + count, h * L : (h + 1) * L] = b["panel_r"][p // 8, (p // 2) % 4, p % 2, inside : inside + count, :]
                    row += count

    for h, b in enumerate(chains):
        split_row_panel(b["panel_r"], b["vcat"])

        @pl.loop(0, 4)
        def _(j, b=b, h=h):
            rows = pl.ds(pl.multiple_of(j * 384, 384), 384)
            high, low = split(product(s["tra_h"], s["tra_l"], b["vcat"], j))
            s["img_h"][rows, h * L : (h + 1) * L] = high
            s["img_l"][rows, h * L : (h + 1) * L] = low
            high, low = split(b["panel_f"][j].reshape(384, L).T)
            s["ft_h"][h * L : (h + 1) * L, rows] = high
            s["ft_l"][h * L : (h + 1) * L, rows] = low

    def inner(p, q):
        return jnp.dot(p[...], q[...], preferred_element_type=F32)

    part = inner(s["ft_h"], s["img_h"]) + (inner(s["ft_h"], s["img_l"]) + inner(s["ft_l"], s["img_h"]))
    red_p["a"][...] = part.reshape(2, 4, 4, 8, 256)
    run([all_sum(me, links[3], red_p)])
    gram[...] = red_g["total"][...].reshape(256, 256)
    projected[...] = red_p["total"][...].reshape(256, 256)


def body(laplacian, block, bounds):
    vmem = pl.BlockSpec(memory_space=pltpu.VMEM)
    scratch = [pltpu.VMEM(shape, kind) for group in (SHARED, CHAIN, CHAIN, REDUCE, REDUCE) for shape, kind in group.values()]
    scratch.append(pltpu.SemaphoreType.DMA)
    for count in (CHAIN_SEMS, CHAIN_SEMS, REDUCE_SEMS, REDUCE_SEMS):
        scratch += [pltpu.SemaphoreType.DMA((count,)), pltpu.SemaphoreType.DMA((count,))]
    square = jax.ShapeDtypeStruct((256, 256), F32)
    filtered, gram, projected = pl.pallas_call(
        body_kernel,
        out_shape=(jax.ShapeDtypeStruct(block.shape, F32), square, square),
        in_specs=[pl.BlockSpec(memory_space=pl.ANY), vmem, pl.BlockSpec(memory_space=pltpu.SMEM)],
        out_specs=(vmem, vmem, vmem),
        scratch_shapes=scratch,
        compiler_params=pltpu.CompilerParams(collective_id=0, has_side_effects=True, vmem_limit_bytes=62 * 1024 * 1024),
        name="filter",
    )(laplacian, block, bounds)
    center = (bounds[1] + bounds[0]) * 0.5
    projected = projected + center * gram
    projected = (projected + projected.T) * 0.5
    factor = jnp.linalg.cholesky(gram)
    first_solve = jax.scipy.linalg.solve_triangular(factor, projected, lower=True)
    rayleigh = jax.scipy.linalg.solve_triangular(factor, first_solve.T, lower=True)
    return filtered, rayleigh


def solution(mesh):
    placed = (P("row", "col"), P(("row", "col"), None), P())
    return jax.shard_map(
        body, mesh=mesh, in_specs=placed, out_specs=(P(("row", "col"), None), P()), check_vma=False
    )
```

```python
import jax
import jax.numpy as jnp
from jax import lax
from jax.experimental import pallas as pl
from jax.experimental.pallas import tpu as pltpu
from jax.sharding import PartitionSpec as P

MESH = pl.DeviceIdType.MESH
F32 = jnp.float32
BF16 = jnp.bfloat16
L = 128
TILE = 1440
PAD = 1536
PIECE = 96
OWN = 90
LEAD = 8

CHAIN = dict(
    raw0=((2, 4, 2, PIECE, L), F32),
    panel0=((PAD, L), F32),
    panel_r=((2, 4, 2, PIECE, L), F32),
    panel_c=((4, 4, 2, 48, L), F32),
    panel_f=((4, 4, 2, 48, L), F32),
    part_c=((4, 4, 2, 48, L), F32),
    part_r=((2, 4, 2, PIECE, L), F32),
    vcat=((PAD, 2 * L), BF16),
    core_in=((4, 2, PIECE, L), F32),
    y_in=((6, 2, 2, 48, L), F32),
    y_sum=((4, 2, 48, L), F32),
    z_in=((3, 2, 48, L), F32),
    x_in=((6, PIECE, L), F32),
    x_sum=((2, PIECE, L), F32),
    h_in=((2, 2, PIECE, L), F32),
    z1=((2, 48, L), F32),
    z2=((2, PIECE, L), F32),
    z4=((2, 48, L), F32),
)
REDUCE = dict(
    a=((2, 4, 4, 8, 256), F32),
    total=((2, 4, 4, 8, 256), F32),
    core_in=((4, 4, 8, 256), F32),
    x_in=((3, 4, 8, 256), F32),
    y_in=((3, 8, 256), F32),
    z_in=((8, 8, 256), F32),
)
SHARED = dict(
    stage=((TILE, TILE), F32),
    strip=((128, PAD), F32),
    mat_h=((PAD, PAD), BF16),
    mat_l=((PAD, PAD), BF16),
    tra_h=((PAD, PAD), BF16),
    tra_l=((PAD, PAD), BF16),
    own4=((128, 256), F32),
    ft_h=((256, PAD), BF16),
    ft_l=((256, PAD), BF16),
    img_h=((PAD, 256), BF16),
    img_l=((PAD, 256), BF16),
    work=((256, 512), F32),
    done=((256, 512), F32),
)
AT_START, AT_ROW, AT_ROWG, AT_COL, AT_COLG, AT_TURN, AT_LAST, CHAIN_SEMS = 0, 11, 20, 29, 39, 49, 50, 59
REDUCE_SEMS = 21


def split(value):
    high = value.astype(BF16)
    return high, (value - high.astype(F32)).astype(BF16)


def together(*tasks):
    tasks = list(tasks)
    while tasks:
        tasks = [t for t in tasks if next(t, "end") != "end"]
        if tasks:
            yield


def run(*tasks):
    for _ in together(*tasks):
        pass


class Kernel:
    def __init__(self):
        r, c = lax.axis_index("row"), lax.axis_index("col")
        self.r, self.c = r, c
        self.y, self.z = r // 4, r % 4
        self.zh, self.x, self.core = c // 8, (c // 2) % 4, c % 2
        self.pos = self.core * 8 + self.x * 2 + self.zh

    def yn(self, d):
        return ((self.y + d) % 4) * 4 + self.z, self.c

    def zn(self, d):
        return self.y * 4 + (self.z + d) % 4, self.c

    def xn(self, d):
        return self.r, self.zh * 8 + ((self.x + d) % 4) * 2 + self.core

    def zall(self, d):
        at = (self.zh * 4 + self.z + d) % 8
        return self.y * 4 + at % 4, (at // 4) * 8 + self.x * 2 + self.core

    def hn(self):
        return self.r, (1 - self.zh) * 8 + self.x * 2 + self.core

    def cn(self):
        return self.r, self.zh * 8 + self.x * 2 + 1 - self.core

    def turn_to(self):
        return self.pos, self.r

    def turn_from(self):
        r = self.r
        return self.c, (r % 2) * 8 + ((r // 2) % 4) * 2 + r // 8


class Link:
    def __init__(self, send, recv):
        self.send, self.recv, self.open = send, recv, []

    def put(self, src, dst, k, device):
        copy = pltpu.make_async_remote_copy(
            src_ref=src, dst_ref=dst, send_sem=self.send.at[k], recv_sem=self.recv.at[k], device_id=device, device_id_type=MESH
        )
        copy.start()
        self.open.append(copy)

    def got(self, dst, k, device):
        pltpu.make_async_remote_copy(
            src_ref=dst, dst_ref=dst, send_sem=self.send.at[k], recv_sem=self.recv.at[k], device_id=device, device_id_type=MESH
        ).wait_recv()

    def flush(self):
        for copy in self.open:
            copy.wait_send()
        self.open = []


def ring_sum(link, k, i, near, half, box, out, ready, slow):
    a, b, d = (i + 1) % 4, (i + 3) % 4, (i + 2) % 4
    ready(d)
    link.put(half(d, 0), box.at[0], k, near(1))
    link.put(half(d, 1), box.at[1], k + 1, near(3))
    if slow:
        yield
    ready(a)
    link.put(half(a, 1), box.at[2], k + 2, near(1))
    if slow:
        yield
    ready(b)
    link.put(half(b, 0), box.at[3], k + 3, near(3))
    if slow:
        yield
    ready(i)
    yield
    link.got(box.at[0], k, near(3))
    half(a, 0)[...] += box[0]
    link.put(half(a, 0), box.at[4], k + 4, near(1))
    link.got(box.at[1], k + 1, near(1))
    half(b, 1)[...] += box[1]
    link.put(half(b, 1), box.at[5], k + 5, near(3))
    yield
    link.got(box.at[2], k + 2, near(3))
    link.got(box.at[3], k + 3, near(1))
    link.got(box.at[4], k + 4, near(3))
    link.got(box.at[5], k + 5, near(1))
    out(0, half(i, 0)[...] + box[4] + box[3])
    out(1, half(i, 1)[...] + box[2] + box[5])


def gather_start(me, link, k, panel):
    own = panel.at[me.core, me.x, me.zh]
    link.put(own, own, k, me.hn())
    yield
    link.got(panel.at[me.core, me.x, 1 - me.zh], k, me.hn())
    yield from gather_col(me, link, k + 1, panel)


def gather_col(me, link, k, panel):
    core, x = me.core, me.x
    a, b, d = (x + 1) % 4, (x + 3) % 4, (x + 2) % 4
    other = 1 - core

    def put(ref, j, device):
        link.put(ref, ref, k + j, device)

    put(panel.at[core, x, 0], 0, me.xn(1))
    put(panel.at[core, x, 1], 1, me.xn(3))
    put(panel.at[core, x, 1], 2, me.xn(1))
    put(panel.at[core, x, 0], 3, me.xn(3))
    put(panel.at[core, x], 6, me.cn())
    yield
    link.got(panel.at[core, b, 0], k, me.xn(3))
    put(panel.at[core, b, 0], 4, me.xn(1))
    link.got(panel.at[core, a, 1], k + 1, me.xn(1))
    put(panel.at[core, a, 1], 5, me.xn(3))
    yield
    link.got(panel.at[core, b, 1], k + 2, me.xn(3))
    put(panel.at[core, b], 7, me.cn())
    link.got(panel.at[core, a, 0], k + 3, me.xn(1))
    put(panel.at[core, a], 8, me.cn())
    link.got(panel.at[core, d, 0], k + 4, me.xn(3))
    link.got(panel.at[core, d, 1], k + 5, me.xn(1))
    put(panel.at[core, d], 9, me.cn())
    yield
    link.got(panel.at[other, x], k + 6, me.cn())
    link.got(panel.at[other, b], k + 7, me.cn())
    link.got(panel.at[other, a], k + 8, me.cn())
    link.got(panel.at[other, d], k + 9, me.cn())


def gather_row(me, link, k, panel):
    y, z = me.y, me.z
    ya, yb, yd = (y + 1) % 4, (y + 3) % 4, (y + 2) % 4

    def put(ref, j, device):
        link.put(ref, ref, k + j, device)

    for d in (1, 2, 3):
        put(panel.at[y, z], d - 1, me.zn(d))
    yield
    for d in (1, 2, 3):
        link.got(panel.at[y, (z + 4 - d) % 4], k + d - 1, me.zn(4 - d))
    low, high = pl.ds(0, 2), pl.ds(2, 2)
    put(panel.at[y, low], 3, me.yn(1))
    put(panel.at[y, high], 4, me.yn(3))
    put(panel.at[y, high], 5, me.yn(1))
    put(panel.at[y, low], 6, me.yn(3))
    yield
    link.got(panel.at[yb, low], k + 3, me.yn(3))
    put(panel.at[yb, low], 7, me.yn(1))
    link.got(panel.at[ya, high], k + 4, me.yn(1))
    put(panel.at[ya, high], 8, me.yn(3))
    yield
    link.got(panel.at[yb, high], k + 5, me.yn(3))
    link.got(panel.at[ya, low], k + 6, me.yn(1))
    link.got(panel.at[yd, low], k + 7, me.yn(3))
    link.got(panel.at[yd, high], k + 8, me.yn(1))


def split_row_panel(panel, vcat):
    @pl.loop(0, 8)
    def _(i):
        high, low = split(panel[i // 4, i % 4].reshape(2 * PIECE, L))
        rows = pl.ds(pl.multiple_of(i * 192, 192), 192)
        vcat[rows, :L] = high
        vcat[rows, L:] = low


def split_col_panel(panel, vcat):
    @pl.loop(0, 4)
    def _(i):
        high, low = split(panel[i].reshape(384, L))
        rows = pl.ds(pl.multiple_of(i * 384, 384), 384)
        vcat[rows, :L] = high
        vcat[rows, L:] = low


def product(high, low, vcat, chunk):
    rows = pl.ds(pl.multiple_of(chunk * 384, 384), 384)
    wide = jnp.dot(high[rows, :], vcat[...], preferred_element_type=F32)
    rest = jnp.dot(low[rows, :], vcat[:, :L], preferred_element_type=F32)
    return wide[:, :L] + (wide[:, L:] + rest)


def odd_step(me, link, s, b, scale, previous, save):
    split_row_panel(b["panel_r"], b["vcat"]) if previous is not None else None
    part, y_sum, panel = b["part_c"], b["y_sum"], b["panel_c"]
    y, z = me.y, me.z

    def ready(j):
        part[j] = product(s["tra_h"], s["tra_l"], b["vcat"], j).reshape(4, 2, 48, L)

    def out_y(h, value):
        y_sum[pl.ds(2 * h, 2)] = value

    yield from ring_sum(link, AT_ROW, y, me.yn, lambda j, h: part.at[j, pl.ds(2 * h, 2)], b["y_in"], out_y, ready, True)
    box, k = b["z_in"], AT_ROW + 6
    for d in (1, 2, 3):
        link.put(y_sum.at[(z + d) % 4], box.at[d - 1], k + d - 1, me.zn(d))
    yield
    for d in (1, 2, 3):
        link.got(box.at[d - 1], k + d - 1, me.zn(4 - d))
    value = ((y_sum[z] + box[0]) + (box[1] + box[2])) * scale
    if previous is not None:
        value = value - previous[...]
    panel[y, z] = value
    if save is not None:
        save[...] = value
    yield from gather_row(me, link, AT_ROWG, panel)
    link.flush()


def even_sum(me, link, s, b, step, scale, previous, store):
    split_col_panel(b["panel_c"], b["vcat"])
    part, box = b["part_r"], b["core_in"]
    core, x = me.core, me.x
    other, first = 1 - core, 1 - x // 2
    k = AT_COL

    def compute(half, pair):
        value = product(s["mat_h"], s["mat_l"], b["vcat"], half * 2 + pair)
        part[half, pl.ds(2 * pair, 2)] = value.reshape(2, 2, PIECE, L)

    compute(other, first)
    link.put(part.at[other, pl.ds(2 * first, 2)], box.at[pl.ds(2 * first, 2)], k, me.cn())
    last = 1 - first
    yield
    compute(other, last)
    link.put(part.at[other, pl.ds(2 * last, 2)], box.at[pl.ds(2 * last, 2)], k + 1, me.cn())
    yield
    compute(core, first)
    yield
    compute(core, last)
    yield
    turn = []

    def ready(j):
        if len(turn) == 0:
            link.got(box.at[pl.ds(2 * first, 2)], k, me.cn())
        if len(turn) == 1:
            link.got(box.at[pl.ds(2 * last, 2)], k + 1, me.cn())
        turn.append(j)
        part[core, j] += box[j]

    x_sum = b["x_sum"]

    def out_x(h, value):
        x_sum[h] = value

    yield from ring_sum(link, k + 2, x, me.xn, lambda j, h: part.at[core, j, h], b["x_in"], out_x, ready, False)
    link.put(x_sum, b["h_in"].at[step], k + 8 + step, me.hn())
    yield
    link.got(b["h_in"].at[step], k + 8 + step, me.hn())
    store((x_sum[...] + b["h_in"][step]) * scale - previous())


def first_gather(me, link, b):
    yield from gather_start(me, link, AT_START, b["raw0"])
    panel0 = b["panel0"]
    panel0[TILE:, :] = jnp.zeros((PAD - TILE, L), F32)
    for c in range(16):
        panel0[c * OWN : (c + 1) * OWN, :] = b["raw0"][c % 2, (c // 2) % 4, c // 8, :OWN, :]

    @pl.loop(0, 4)
    def _(i):
        rows = pl.ds(pl.multiple_of(i * 384, 384), 384)
        high, low = split(panel0[rows, :])
        b["vcat"][rows, :L] = high
        b["vcat"][rows, L:] = low

    link.flush()


def chain(me, link, s, b, h, half_width, alone, reached):
    one, two = 1.0 / half_width, 2.0 / half_width
    yield from odd_step(me, link, s, b, one, None, b["z1"])
    panel0, z2, panel_r = b["panel0"], b["z2"], b["panel_r"]

    def store2(value):
        z2[...] = value
        panel_r[me.core, me.x] = value

    rows = pl.ds(pl.multiple_of((me.core * 4 + me.x) * 192, 192), 192)
    yield from even_sum(me, link, s, b, 0, two, lambda: panel0[rows, :].reshape(2, PIECE, L), store2)
    yield from gather_col(me, link, AT_COLG, panel_r)
    link.flush()
    yield from odd_step(me, link, s, b, two, b["z1"], None)

    def store4(value):
        panel_r[me.core, me.x] = value

    yield from even_sum(me, link, s, b, 1, two, lambda: z2[...], store4)
    link.flush()
    b["z4"][...] = panel_r[me.core, me.x, me.zh].reshape(2, 48, L)
    s["own4"][:PIECE, h * L : (h + 1) * L] = b["z4"][...].reshape(PIECE, L)
    reached.append("block")
    yield from together(gather_col(me, link, AT_COLG, panel_r), turned_gather(me, link, b, alone))
    link.flush()
    split_row_panel(panel_r, b["vcat"])
    for j in range(4):
        rows = slice(j * 384, (j + 1) * 384)
        high, low = split(product(s["tra_h"], s["tra_l"], b["vcat"], j))
        s["img_h"][rows, h * L : (h + 1) * L] = high
        s["img_l"][rows, h * L : (h + 1) * L] = low
        high, low = split(b["panel_f"][j].reshape(384, L).T)
        s["ft_h"][h * L : (h + 1) * L, rows] = high
        s["ft_l"][h * L : (h + 1) * L, rows] = low
        yield
    reached.append("image")


def turned_gather(me, link, b, alone):
    panel, z4 = b["panel_f"], b["z4"]
    row, col = me.turn_to()
    slot = panel.at[row // 4, row % 4]

    def copy():
        return pltpu.make_async_remote_copy(
            src_ref=z4,
            dst_ref=slot,
            send_sem=link.send.at[AT_TURN],
            recv_sem=link.recv.at[AT_TURN],
            device_id=(row, col),
            device_id_type=MESH,
        )

    @pl.when(jnp.logical_not(alone))
    def _():
        copy().start()

    @pl.when(alone)
    def _():
        panel[me.y, me.z] = z4[...]

    yield

    @pl.when(jnp.logical_not(alone))
    def _():
        link.got(panel.at[me.y, me.z], AT_TURN, me.turn_from())
        copy().wait_send()

    yield from gather_row(me, link, AT_LAST, panel)


def all_sum(me, link, b):
    a, total = b["a"], b["total"]
    y, z, x, core = me.y, me.z, me.x, me.core
    other = 1 - core
    link.put(a.at[other], b["core_in"], 0, me.cn())
    yield
    link.got(b["core_in"], 0, me.cn())
    a[core] += b["core_in"][...]
    for d in (1, 2, 3):
        link.put(a.at[core, (x + d) % 4], b["x_in"].at[d - 1], d, me.xn(d))
    yield
    for d in (1, 2, 3):
        link.got(b["x_in"].at[d - 1], d, me.xn(4 - d))
    a[core, x] += (b["x_in"][0] + b["x_in"][1]) + b["x_in"][2]
    for d in (1, 2, 3):
        link.put(a.at[core, x, (y + d) % 4], b["y_in"].at[d - 1], 3 + d, me.yn(d))
    yield
    for d in (1, 2, 3):
        link.got(b["y_in"].at[d - 1], 3 + d, me.yn(4 - d))
    at = me.zh * 4 + z
    box = b["z_in"]
    box[at] = a[core, x, y] + ((b["y_in"][0] + b["y_in"][1]) + b["y_in"][2])
    for d in range(1, 8):
        link.put(box.at[at], box.at[at], 6 + d, me.zall(d))
    yield
    for d in range(1, 8):
        link.got(box.at[(at + 8 - d) % 8], 6 + d, me.zall(8 - d))
    total[core, x, y] = ((box[0] + box[1]) + (box[2] + box[3])) + ((box[4] + box[5]) + (box[6] + box[7]))
    for d in (1, 2, 3):
        link.put(total.at[core, x, y], total.at[core, x, y], 13 + d, me.yn(d))
    yield
    for d in (1, 2, 3):
        link.got(total.at[core, x, (y + 4 - d) % 4], 13 + d, me.yn(4 - d))
    for d in (1, 2, 3):
        link.put(total.at[core, x], total.at[core, x], 16 + d, me.xn(d))
    yield
    for d in (1, 2, 3):
        link.got(total.at[core, (x + 4 - d) % 4], 16 + d, me.xn(4 - d))
    link.put(total.at[core], total.at[core], 20, me.cn())
    yield
    link.got(total.at[other], 20, me.cn())
    link.flush()


BLOCK = 64
GROUPS = BLOCK // 8


def eliminate(groups, turn):
    row = lax.broadcasted_iota(jnp.int32, (8, 128), 0)
    wide = (8, 128)

    def sub(value, j):
        return jnp.broadcast_to(value[j : j + 1, :], wide)

    for j in range(0, 8, 2):
        col0 = [jnp.broadcast_to(g[:, j : j + 1], wide) for g in groups]
        col1 = [jnp.broadcast_to(g[:, j + 1 : j + 2], wide) for g in groups]
        inv0 = 1.0 / sub(col0[0], j)
        lower = sub(col0[0], j + 1) * inv0
        upper = sub(col1[0], j)
        inv1 = 1.0 / (sub(col1[0], j + 1) - lower * upper)
        row0 = sub(groups[0], j)
        row1 = sub(groups[0], j + 1) - lower * row0
        for g in range(GROUPS):
            mul0 = col0[g] * inv0
            mul1 = (col1[g] - mul0 * upper) * inv1
            if g == 0:
                mul0 = jnp.where(row > j, mul0, 0.0)
                mul1 = jnp.where(row > j + 1, mul1, 0.0)
            else:
                left = turn + g < GROUPS
                mul0 = jnp.where(left, mul0, 0.0)
                mul1 = jnp.where(left, mul1, 0.0)
            groups[g] = groups[g] - mul0 * row0 - mul1 * row1
    return [pltpu.roll(g, 120, 1) for g in groups[1:] + groups[:1]]


def exact(p, q, dims):
    return lax.dot_general(p, q, (dims, ((), ())), precision=lax.Precision.HIGHEST, preferred_element_type=F32)


def invert_factor(s, gram):
    work, done = s["work"], s["done"]
    row = lax.broadcasted_iota(jnp.int32, (256, 256), 0)
    col = lax.broadcasted_iota(jnp.int32, (256, 256), 1)
    work[:, :256] = gram
    work[:, 256:] = jnp.where(row == col, 1.0, 0.0)
    small_row = lax.broadcasted_iota(jnp.int32, (BLOCK, 128), 0)
    small_col = lax.broadcasted_iota(jnp.int32, (BLOCK, 128), 1)
    for b in range(256 // BLOCK):
        rows = slice(b * BLOCK, (b + 1) * BLOCK)
        lanes = b * BLOCK // 128 * 128
        block = work[rows, lanes : lanes + 128]
        if b % 2:
            block = pltpu.roll(block, 64, 1)
        block = jnp.where(small_col < BLOCK, block, jnp.where(small_col == small_row + BLOCK, 1.0, 0.0))
        groups = tuple(block[8 * g : 8 * g + 8] for g in range(GROUPS))
        for half in range(2):
            at = half * GROUPS // 2
            groups = lax.fori_loop(at, at + GROUPS // 2, lambda i, gs: tuple(eliminate(list(gs), i)), groups)
            yield
        block = jnp.concatenate(groups, axis=0)
        pivot = jnp.sum(jnp.where(small_col == small_row + BLOCK, block, 0.0), axis=1, keepdims=True)
        root = lax.rsqrt(pivot)
        root = root * (1.5 - 0.5 * pivot * root * root)
        inverse = (block * root)[:, :BLOCK]
        mine = exact(inverse, work[rows, :], ((1,), (0,)))
        done[rows, :] = mine
        if b < 256 // BLOCK - 1:
            after = exact(mine[:, :256], mine, ((0,), (0,)))
            work[(b + 1) * BLOCK :, :] -= after[(b + 1) * BLOCK :, :]
        yield


def gram_task(me, link, s, b, reached):
    while reached.count("block") < 2:
        yield
    high, low = split(s["own4"][...])
    dims = (((0,), (0,)), ((), ()))

    def pair(p, q):
        return lax.dot_general(p, q, dims, preferred_element_type=F32)

    part = pair(high, high) + (pair(high, low) + pair(low, high))
    b["a"][...] = part.reshape(2, 4, 4, 8, 256)
    yield from all_sum(me, link, b)
    yield from invert_factor(s, b["total"][...].reshape(256, 256))


def projected_task(me, link, s, b, reached):
    while reached.count("image") < 2:
        yield

    def inner(p, q):
        return jnp.dot(p[...], q[...], preferred_element_type=F32)

    part = inner(s["ft_h"], s["img_h"]) + (inner(s["ft_h"], s["img_l"]) + inner(s["ft_l"], s["img_h"]))
    b["a"][...] = part.reshape(2, 4, 4, 8, 256)
    yield from all_sum(me, link, b)


def body_kernel(lap, block, bounds, filtered, rayleigh, *scratch):
    names = list(SHARED), list(CHAIN), list(CHAIN), list(REDUCE), list(REDUCE)
    groups, at = [], 0
    for group in names:
        groups.append(dict(zip(group, scratch[at : at + len(group)])))
        at += len(group)
    s, *chains, red_g, red_p = groups
    lap_sem, *sems = scratch[at:]
    links = [Link(sems[2 * i], sems[2 * i + 1]) for i in range(4)]
    me = Kernel()
    to_row, to_col = me.turn_to()
    alone = jnp.logical_and(to_row == me.r, to_col == me.c)

    load = pltpu.make_async_copy(lap, s["stage"], lap_sem)
    load.start()
    for h, b in enumerate(chains):
        own = b["raw0"].at[me.core, me.x, me.zh]
        own[OWN - 2 :, :] = jnp.zeros((PIECE - OWN + 2, L), F32)
        own[:OWN, :] = block[:, h * L : (h + 1) * L]

    barrier = pltpu.get_barrier_semaphore()
    near = [f(d) for f in (me.yn, me.xn) for d in (1, 2, 3)] + [me.zall(d) for d in range(1, 8)] + [me.cn()]
    for device in near:
        pl.semaphore_signal(barrier, inc=1, device_id=device, device_id_type=MESH)

    @pl.when(jnp.logical_not(alone))
    def _():
        pl.semaphore_signal(barrier, inc=1, device_id=me.turn_to(), device_id_type=MESH)
        pl.semaphore_signal(barrier, inc=1, device_id=me.turn_from(), device_id_type=MESH)

    pl.semaphore_wait(barrier, jnp.where(alone, len(near), len(near) + 2))

    center = (bounds[1] + bounds[0]) * 0.5
    half_width = (bounds[1] - bounds[0]) * 0.5

    def prepare():
        load.wait()
        shift = jnp.where(me.r == me.c, center, 0.0)
        strip = s["strip"]
        strip[...] = jnp.zeros_like(strip)

        def strip_of(start, count):
            value = s["stage"][pl.ds(start, count), :]
            row = start + lax.broadcasted_iota(jnp.int32, (count, TILE), 0)
            col = lax.broadcasted_iota(jnp.int32, (count, TILE), 1)
            strip[:count, :TILE] = value - jnp.where(row == col, shift, 0.0)

        def spread(start):
            whole = strip[...]
            high, low = split(whole)
            s["mat_h"][pl.ds(start, 128), :] = high
            s["mat_l"][pl.ds(start, 128), :] = low
            high, low = split(whole.T)
            s["tra_h"][:, pl.ds(start, 128)] = high
            s["tra_l"][:, pl.ds(start, 128)] = low

        for at in (0, 3, 6, 9):

            @pl.loop(at, min(at + 3, TILE // 128))
            def _(i):
                start = pl.multiple_of(i * 128, 128)
                strip_of(start, 128)
                spread(start)

            yield

        strip[...] = jnp.zeros_like(strip)
        strip_of(TILE // 128 * 128, TILE % 128)
        spread(TILE // 128 * 128)

    s["own4"][PIECE:, :] = jnp.zeros((128 - PIECE, 256), F32)
    reached = []
    one, two = (chain(me, links[h], s, chains[h], h, half_width, alone, reached) for h in (0, 1))
    start = [first_gather(me, links[h], chains[h]) for h in (0, 1)]
    run(start[0], prepare())
    late = together(start[1])
    for _ in range(LEAD):
        next(one)
        next(late, None)

    def second():
        yield from late
        yield from two

    run(one, second(), gram_task(me, links[2], s, red_g, reached), projected_task(me, links[3], s, red_p, reached))
    for c in range(16):

        @pl.when(me.c == c)
        def _(c=c):
            for h, b in enumerate(chains):
                row = 0
                while row < OWN:
                    at = c * OWN + row
                    p, inside = at // PIECE, at % PIECE
                    count = min(PIECE - inside, OWN - row)
                    filtered[row : row + count, h * L : (h + 1) * L] = b["panel_r"][p // 8, (p // 2) % 4, p % 2, inside : inside + count, :]
                    row += count

    projected = red_p["total"][...].reshape(256, 256) + center * red_g["total"][...].reshape(256, 256)
    projected = (projected + projected.T) * 0.5
    inverse = s["done"][:, 256:]
    rayleigh[...] = exact(exact(inverse, projected, ((1,), (0,))), inverse, ((1,), (1,)))


def body(laplacian, block, bounds):
    vmem = pl.BlockSpec(memory_space=pltpu.VMEM)
    scratch = [pltpu.VMEM(shape, kind) for group in (SHARED, CHAIN, CHAIN, REDUCE, REDUCE) for shape, kind in group.values()]
    scratch.append(pltpu.SemaphoreType.DMA)
    for count in (CHAIN_SEMS, CHAIN_SEMS, REDUCE_SEMS, REDUCE_SEMS):
        scratch += [pltpu.SemaphoreType.DMA((count,)), pltpu.SemaphoreType.DMA((count,))]
    return pl.pallas_call(
        body_kernel,
        out_shape=(jax.ShapeDtypeStruct(block.shape, F32), jax.ShapeDtypeStruct((256, 256), F32)),
        in_specs=[pl.BlockSpec(memory_space=pl.ANY), vmem, pl.BlockSpec(memory_space=pltpu.SMEM)],
        out_specs=(vmem, vmem),
        scratch_shapes=scratch,
        compiler_params=pltpu.CompilerParams(collective_id=0, has_side_effects=True, vmem_limit_bytes=62 * 1024 * 1024),
        name="filter",
    )(laplacian, block, bounds)


def solution(mesh):
    placed = (P("row", "col"), P(("row", "col"), None), P())
    return jax.shard_map(
        body, mesh=mesh, in_specs=placed, out_specs=(P(("row", "col"), None), P()), check_vma=False
    )
```

```python
import jax
import jax.numpy as jnp
from jax import lax
from jax.experimental import pallas as pl
from jax.experimental.pallas import tpu as pltpu
from jax.sharding import PartitionSpec as P

MESH = pl.DeviceIdType.MESH
F32 = jnp.float32
BF16 = jnp.bfloat16
L = 128
TILE = 1440
PAD = 1536
PIECE = 96
OWN = 90

CHAIN = dict(
    raw0=((2, 4, 2, PIECE, L), F32),
    panel0=((PAD, L), F32),
    panel_r=((2, 4, 2, PIECE, L), F32),
    panel_c=((4, 4, 2, 48, L), F32),
    panel_f=((4, 4, 2, 48, L), F32),
    part_c=((4, 4, 2, 48, L), F32),
    part_r=((2, 4, 2, PIECE, L), F32),
    vcat=((PAD, 2 * L), BF16),
    core_in=((4, 2, PIECE, L), F32),
    y_in=((6, 2, 2, 48, L), F32),
    y_sum=((4, 2, 48, L), F32),
    z_in=((3, 2, 48, L), F32),
    x_in=((6, PIECE, L), F32),
    x_sum=((2, PIECE, L), F32),
    h_in=((2, 2, PIECE, L), F32),
    z1=((2, 48, L), F32),
    z2=((2, PIECE, L), F32),
    z4=((2, 48, L), F32),
)
def reduce_of(piece):
    cut = (4, *piece) if piece[0] == 8 else piece
    return dict(
        a=((2, 4, *cut), F32),
        total=((2, 4, *cut), F32),
        core_in=((4, *cut), F32),
        x_in=((3, *cut), F32),
        y_in=((4, *piece), F32),
        z_in=((8, *piece), F32),
    )


REDUCES = reduce_of((16, L)), reduce_of((8, L)), reduce_of((8, 256))
SHARED = dict(
    stage=((TILE, TILE), F32),
    strip=((128, PAD), F32),
    mat_h=((PAD, PAD), BF16),
    mat_l=((PAD, PAD), BF16),
    tra_h=((PAD, PAD), BF16),
    tra_l=((PAD, PAD), BF16),
    own4=((128, 256), F32),
    ft_h=((256, PAD), BF16),
    ft_l=((256, PAD), BF16),
    img_h=((PAD, 256), BF16),
    img_l=((PAD, 256), BF16),
    work=((L, 256), F32),
    done0=((L, 256), F32),
    done1=((L, 256), F32),
    inverse=((256, 256), F32),
    gram=((256, 256), F32),
)
AT_START, AT_ROW, AT_ROWG, AT_COL, AT_COLG, AT_TURN, AT_LAST, CHAIN_SEMS = 0, 11, 20, 29, 39, 49, 50, 59
REDUCE_SEMS = 21


def split(value):
    high = value.astype(BF16)
    return high, (value - high.astype(F32)).astype(BF16)


def together(*tasks):
    tasks = list(tasks)
    while tasks:
        tasks = [t for t in tasks if next(t, "end") != "end"]
        if tasks:
            yield


def run(*tasks):
    for _ in together(*tasks):
        pass


class Kernel:
    def __init__(self):
        r, c = lax.axis_index("row"), lax.axis_index("col")
        self.r, self.c = r, c
        self.y, self.z = r // 4, r % 4
        self.zh, self.x, self.core = c // 8, (c // 2) % 4, c % 2
        self.pos = self.core * 8 + self.x * 2 + self.zh

    def yn(self, d):
        return ((self.y + d) % 4) * 4 + self.z, self.c

    def zn(self, d):
        return self.y * 4 + (self.z + d) % 4, self.c

    def xn(self, d):
        return self.r, self.zh * 8 + ((self.x + d) % 4) * 2 + self.core

    def zall(self, d):
        at = (self.zh * 4 + self.z + d) % 8
        return self.y * 4 + at % 4, (at // 4) * 8 + self.x * 2 + self.core

    def hn(self):
        return self.r, (1 - self.zh) * 8 + self.x * 2 + self.core

    def cn(self):
        return self.r, self.zh * 8 + self.x * 2 + 1 - self.core

    def turn_to(self):
        return self.pos, self.r

    def turn_from(self):
        r = self.r
        return self.c, (r % 2) * 8 + ((r // 2) % 4) * 2 + r // 8


class Link:
    def __init__(self, send, recv):
        self.send, self.recv, self.open = send, recv, []

    def put(self, src, dst, k, device):
        copy = pltpu.make_async_remote_copy(
            src_ref=src, dst_ref=dst, send_sem=self.send.at[k], recv_sem=self.recv.at[k], device_id=device, device_id_type=MESH
        )
        copy.start()
        self.open.append(copy)

    def got(self, dst, k, device):
        pltpu.make_async_remote_copy(
            src_ref=dst, dst_ref=dst, send_sem=self.send.at[k], recv_sem=self.recv.at[k], device_id=device, device_id_type=MESH
        ).wait_recv()

    def flush(self):
        for copy in self.open:
            copy.wait_send()
        self.open = []


def ring_sum(link, k, i, near, half, box, out, ready):
    a, b, d = (i + 1) % 4, (i + 3) % 4, (i + 2) % 4
    ready(d)
    link.put(half(d, 0), box.at[0], k, near(1))
    link.put(half(d, 1), box.at[1], k + 1, near(3))
    ready(a)
    link.put(half(a, 1), box.at[2], k + 2, near(1))
    ready(b)
    link.put(half(b, 0), box.at[3], k + 3, near(3))
    ready(i)
    yield
    link.got(box.at[0], k, near(3))
    half(a, 0)[...] += box[0]
    link.put(half(a, 0), box.at[4], k + 4, near(1))
    link.got(box.at[1], k + 1, near(1))
    half(b, 1)[...] += box[1]
    link.put(half(b, 1), box.at[5], k + 5, near(3))
    yield
    link.got(box.at[2], k + 2, near(3))
    link.got(box.at[3], k + 3, near(1))
    link.got(box.at[4], k + 4, near(3))
    link.got(box.at[5], k + 5, near(1))
    out(0, half(i, 0)[...] + box[4] + box[3])
    out(1, half(i, 1)[...] + box[2] + box[5])


def gather_start(me, link, k, panel):
    own = panel.at[me.core, me.x, me.zh]
    link.put(own, own, k, me.hn())
    yield
    link.got(panel.at[me.core, me.x, 1 - me.zh], k, me.hn())
    yield from gather_col(me, link, k + 1, panel)


def gather_col(me, link, k, panel):
    core, x = me.core, me.x
    a, b, d = (x + 1) % 4, (x + 3) % 4, (x + 2) % 4
    other = 1 - core

    def put(ref, j, device):
        link.put(ref, ref, k + j, device)

    put(panel.at[core, x, 0], 0, me.xn(1))
    put(panel.at[core, x, 1], 1, me.xn(3))
    put(panel.at[core, x, 1], 2, me.xn(1))
    put(panel.at[core, x, 0], 3, me.xn(3))
    put(panel.at[core, x], 6, me.cn())
    yield
    link.got(panel.at[core, b, 0], k, me.xn(3))
    put(panel.at[core, b, 0], 4, me.xn(1))
    link.got(panel.at[core, a, 1], k + 1, me.xn(1))
    put(panel.at[core, a, 1], 5, me.xn(3))
    yield
    link.got(panel.at[core, b, 1], k + 2, me.xn(3))
    put(panel.at[core, b], 7, me.cn())
    link.got(panel.at[core, a, 0], k + 3, me.xn(1))
    put(panel.at[core, a], 8, me.cn())
    link.got(panel.at[core, d, 0], k + 4, me.xn(3))
    link.got(panel.at[core, d, 1], k + 5, me.xn(1))
    put(panel.at[core, d], 9, me.cn())
    yield
    link.got(panel.at[other, x], k + 6, me.cn())
    link.got(panel.at[other, b], k + 7, me.cn())
    link.got(panel.at[other, a], k + 8, me.cn())
    link.got(panel.at[other, d], k + 9, me.cn())


def gather_row(me, link, k, panel):
    y, z = me.y, me.z
    ya, yb, yd = (y + 1) % 4, (y + 3) % 4, (y + 2) % 4

    def put(ref, j, device):
        link.put(ref, ref, k + j, device)

    for d in (1, 2, 3):
        put(panel.at[y, z], d - 1, me.zn(d))
    yield
    for d in (1, 2, 3):
        link.got(panel.at[y, (z + 4 - d) % 4], k + d - 1, me.zn(4 - d))
    low, high = pl.ds(0, 2), pl.ds(2, 2)
    put(panel.at[y, low], 3, me.yn(1))
    put(panel.at[y, high], 4, me.yn(3))
    put(panel.at[y, high], 5, me.yn(1))
    put(panel.at[y, low], 6, me.yn(3))
    yield
    link.got(panel.at[yb, low], k + 3, me.yn(3))
    put(panel.at[yb, low], 7, me.yn(1))
    link.got(panel.at[ya, high], k + 4, me.yn(1))
    put(panel.at[ya, high], 8, me.yn(3))
    yield
    link.got(panel.at[yb, high], k + 5, me.yn(3))
    link.got(panel.at[ya, low], k + 6, me.yn(1))
    link.got(panel.at[yd, low], k + 7, me.yn(3))
    link.got(panel.at[yd, high], k + 8, me.yn(1))


def split_row_panel(panel, vcat):
    @pl.loop(0, 8)
    def _(i):
        high, low = split(panel[i // 4, i % 4].reshape(2 * PIECE, L))
        rows = pl.ds(pl.multiple_of(i * 192, 192), 192)
        vcat[rows, :L] = high
        vcat[rows, L:] = low


def split_col_panel(panel, vcat):
    @pl.loop(0, 4)
    def _(i):
        high, low = split(panel[i].reshape(384, L))
        rows = pl.ds(pl.multiple_of(i * 384, 384), 384)
        vcat[rows, :L] = high
        vcat[rows, L:] = low


def product(high, low, vcat, chunk):
    rows = pl.ds(pl.multiple_of(chunk * 384, 384), 384)
    wide = jnp.dot(high[rows, :], vcat[...], preferred_element_type=F32)
    rest = jnp.dot(low[rows, :], vcat[:, :L], preferred_element_type=F32)
    return wide[:, :L] + (wide[:, L:] + rest)


def odd_step(me, link, s, b, scale, previous, save):
    split_row_panel(b["panel_r"], b["vcat"]) if previous is not None else None
    part, y_sum, panel = b["part_c"], b["y_sum"], b["panel_c"]
    y, z = me.y, me.z

    def ready(j):
        part[j] = product(s["tra_h"], s["tra_l"], b["vcat"], j).reshape(4, 2, 48, L)

    def out_y(h, value):
        y_sum[pl.ds(2 * h, 2)] = value

    yield from ring_sum(link, AT_ROW, y, me.yn, lambda j, h: part.at[j, pl.ds(2 * h, 2)], b["y_in"], out_y, ready)
    box, k = b["z_in"], AT_ROW + 6
    for d in (1, 2, 3):
        link.put(y_sum.at[(z + d) % 4], box.at[d - 1], k + d - 1, me.zn(d))
    yield
    for d in (1, 2, 3):
        link.got(box.at[d - 1], k + d - 1, me.zn(4 - d))
    value = ((y_sum[z] + box[0]) + (box[1] + box[2])) * scale
    if previous is not None:
        value = value - previous[...]
    panel[y, z] = value
    if save is not None:
        save[...] = value
    yield from gather_row(me, link, AT_ROWG, panel)
    link.flush()


def even_sum(me, link, s, b, step, scale, previous, store):
    split_col_panel(b["panel_c"], b["vcat"])
    part, box = b["part_r"], b["core_in"]
    core, x = me.core, me.x
    other, first = 1 - core, 1 - x // 2
    k = AT_COL

    def compute(half, pair):
        value = product(s["mat_h"], s["mat_l"], b["vcat"], half * 2 + pair)
        part[half, pl.ds(2 * pair, 2)] = value.reshape(2, 2, PIECE, L)

    compute(other, first)
    link.put(part.at[other, pl.ds(2 * first, 2)], box.at[pl.ds(2 * first, 2)], k, me.cn())
    last = 1 - first
    compute(other, last)
    link.put(part.at[other, pl.ds(2 * last, 2)], box.at[pl.ds(2 * last, 2)], k + 1, me.cn())
    compute(core, first)
    compute(core, last)
    yield
    turn = []

    def ready(j):
        if len(turn) == 0:
            link.got(box.at[pl.ds(2 * first, 2)], k, me.cn())
        if len(turn) == 1:
            link.got(box.at[pl.ds(2 * last, 2)], k + 1, me.cn())
        turn.append(j)
        part[core, j] += box[j]

    x_sum = b["x_sum"]

    def out_x(h, value):
        x_sum[h] = value

    yield from ring_sum(link, k + 2, x, me.xn, lambda j, h: part.at[core, j, h], b["x_in"], out_x, ready)
    link.put(x_sum, b["h_in"].at[step], k + 8 + step, me.hn())
    yield
    link.got(b["h_in"].at[step], k + 8 + step, me.hn())
    store((x_sum[...] + b["h_in"][step]) * scale - previous())


def first_gather(me, link, b):
    yield from gather_start(me, link, AT_START, b["raw0"])
    panel0 = b["panel0"]
    panel0[TILE:, :] = jnp.zeros((PAD - TILE, L), F32)
    for c in range(16):
        panel0[c * OWN : (c + 1) * OWN, :] = b["raw0"][c % 2, (c // 2) % 4, c // 8, :OWN, :]

    @pl.loop(0, 4)
    def _(i):
        rows = pl.ds(pl.multiple_of(i * 384, 384), 384)
        high, low = split(panel0[rows, :])
        b["vcat"][rows, :L] = high
        b["vcat"][rows, L:] = low

    link.flush()


def chain(me, link, s, b, h, half_width, alone, reached):
    one, two = 1.0 / half_width, 2.0 / half_width
    yield from odd_step(me, link, s, b, one, None, b["z1"])
    panel0, z2, panel_r = b["panel0"], b["z2"], b["panel_r"]

    def store2(value):
        z2[...] = value
        panel_r[me.core, me.x] = value

    rows = pl.ds(pl.multiple_of((me.core * 4 + me.x) * 192, 192), 192)
    yield from even_sum(me, link, s, b, 0, two, lambda: panel0[rows, :].reshape(2, PIECE, L), store2)
    yield from gather_col(me, link, AT_COLG, panel_r)
    link.flush()
    yield from odd_step(me, link, s, b, two, b["z1"], None)

    def store4(value):
        panel_r[me.core, me.x] = value

    yield from even_sum(me, link, s, b, 1, two, lambda: z2[...], store4)
    link.flush()
    b["z4"][...] = panel_r[me.core, me.x, me.zh].reshape(2, 48, L)
    s["own4"][:PIECE, h * L : (h + 1) * L] = b["z4"][...].reshape(PIECE, L)
    reached.append("block")

    def image():
        yield from gather_col(me, link, AT_COLG, panel_r)
        split_row_panel(panel_r, b["vcat"])
        for j in range(4):
            high, low = split(product(s["tra_h"], s["tra_l"], b["vcat"], j))
            s["img_h"][j * 384 : (j + 1) * 384, h * L : (h + 1) * L] = high
            s["img_l"][j * 384 : (j + 1) * 384, h * L : (h + 1) * L] = low

    def rows_across():
        yield from turned_gather(me, link, b, alone)
        for j in range(4):
            high, low = split(b["panel_f"][j].reshape(384, L).T)
            s["ft_h"][h * L : (h + 1) * L, j * 384 : (j + 1) * 384] = high
            s["ft_l"][h * L : (h + 1) * L, j * 384 : (j + 1) * 384] = low

    yield from together(image(), rows_across())
    link.flush()
    reached.append("image")


def turned_gather(me, link, b, alone):
    panel, z4 = b["panel_f"], b["z4"]
    row, col = me.turn_to()
    slot = panel.at[row // 4, row % 4]

    def copy():
        return pltpu.make_async_remote_copy(
            src_ref=z4,
            dst_ref=slot,
            send_sem=link.send.at[AT_TURN],
            recv_sem=link.recv.at[AT_TURN],
            device_id=(row, col),
            device_id_type=MESH,
        )

    @pl.when(jnp.logical_not(alone))
    def _():
        copy().start()

    @pl.when(alone)
    def _():
        panel[me.y, me.z] = z4[...]

    yield

    @pl.when(jnp.logical_not(alone))
    def _():
        link.got(panel.at[me.y, me.z], AT_TURN, me.turn_from())
        copy().wait_send()

    yield from gather_row(me, link, AT_LAST, panel)


def all_sum(me, link, b):
    a, total = b["a"], b["total"]
    y, z, x, core = me.y, me.z, me.x, me.core
    other = 1 - core
    whole = len(a.shape) == 4
    link.put(a.at[other], b["core_in"], 0, me.cn())
    yield
    link.got(b["core_in"], 0, me.cn())
    a[core] += b["core_in"][...]
    for d in (1, 2, 3):
        link.put(a.at[core, (x + d) % 4], b["x_in"].at[d - 1], d, me.xn(d))
    yield
    for d in (1, 2, 3):
        link.got(b["x_in"].at[d - 1], d, me.xn(4 - d))
    near = a[core, x] + ((b["x_in"][0] + b["x_in"][1]) + b["x_in"][2])
    box = b["y_in"]
    if whole:
        box[y] = near
    else:
        a[core, x] = near
        box[y] = a[core, x, y]
    for d in (1, 2, 3):
        place = (y + d) % 4
        link.put(box.at[y] if whole else a.at[core, x, place], box.at[y], 3 + d, me.yn(d))
    yield
    for d in (1, 2, 3):
        link.got(box.at[(y + 4 - d) % 4], 3 + d, me.yn(4 - d))
    at = me.zh * 4 + z
    near, box = (box[0] + box[1]) + (box[2] + box[3]), b["z_in"]
    box[at] = near
    for d in range(1, 8):
        link.put(box.at[at], box.at[at], 6 + d, me.zall(d))
    yield
    for d in range(1, 8):
        link.got(box.at[(at + 8 - d) % 8], 6 + d, me.zall(8 - d))
    near = ((box[0] + box[1]) + (box[2] + box[3])) + ((box[4] + box[5]) + (box[6] + box[7]))
    if whole:
        total[core, x] = near
    else:
        total[core, x, y] = near
        for d in (1, 2, 3):
            link.put(total.at[core, x, y], total.at[core, x, y], 13 + d, me.yn(d))
        yield
        for d in (1, 2, 3):
            link.got(total.at[core, x, (y + 4 - d) % 4], 13 + d, me.yn(4 - d))
    for d in (1, 2, 3):
        link.put(total.at[core, x], total.at[core, x], 16 + d, me.xn(d))
    yield
    for d in (1, 2, 3):
        link.got(total.at[core, (x + 4 - d) % 4], 16 + d, me.xn(4 - d))
    link.put(total.at[core], total.at[core], 20, me.cn())
    yield
    link.got(total.at[other], 20, me.cn())
    link.flush()


BLOCK = 64
GROUPS = BLOCK // 8


def eliminate(groups, turn):
    row = lax.broadcasted_iota(jnp.int32, (8, 128), 0)
    wide = (8, 128)

    def sub(value, j):
        return jnp.broadcast_to(value[j : j + 1, :], wide)

    for j in range(0, 8, 2):
        col0 = [jnp.broadcast_to(g[:, j : j + 1], wide) for g in groups]
        col1 = [jnp.broadcast_to(g[:, j + 1 : j + 2], wide) for g in groups]
        inv0 = 1.0 / sub(col0[0], j)
        lower = sub(col0[0], j + 1) * inv0
        upper = sub(col1[0], j)
        inv1 = 1.0 / (sub(col1[0], j + 1) - lower * upper)
        row0 = sub(groups[0], j)
        row1 = sub(groups[0], j + 1) - lower * row0
        for g in range(GROUPS):
            mul0 = col0[g] * inv0
            mul1 = (col1[g] - mul0 * upper) * inv1
            if g == 0:
                mul0 = jnp.where(row > j, mul0, 0.0)
                mul1 = jnp.where(row > j + 1, mul1, 0.0)
            else:
                left = turn + g < GROUPS
                mul0 = jnp.where(left, mul0, 0.0)
                mul1 = jnp.where(left, mul1, 0.0)
            groups[g] = groups[g] - mul0 * row0 - mul1 * row1
    return [pltpu.roll(g, 120, 1) for g in groups[1:] + groups[:1]]


def exact(p, q, dims):
    return lax.dot_general(p, q, (dims, ((), ())), precision=lax.Precision.HIGHEST, preferred_element_type=F32)


def invert_factor(work, done, gram):
    row = lax.broadcasted_iota(jnp.int32, (L, L), 0)
    col = lax.broadcasted_iota(jnp.int32, (L, L), 1)
    work[:, :L] = gram
    work[:, L:] = jnp.where(row == col, 1.0, 0.0)
    row = lax.broadcasted_iota(jnp.int32, (BLOCK, L), 0)
    col = lax.broadcasted_iota(jnp.int32, (BLOCK, L), 1)
    for b in range(L // BLOCK):
        rows = slice(b * BLOCK, (b + 1) * BLOCK)
        block = work[rows, :L]
        if b % 2:
            block = pltpu.roll(block, 64, 1)
        block = jnp.where(col < BLOCK, block, jnp.where(col == row + BLOCK, 1.0, 0.0))
        groups = tuple(block[8 * g : 8 * g + 8] for g in range(GROUPS))
        for half in range(2):
            at = half * GROUPS // 2
            groups = lax.fori_loop(at, at + GROUPS // 2, lambda i, gs: tuple(eliminate(list(gs), i)), groups)
            yield
        block = jnp.concatenate(groups, axis=0)
        pivot = jnp.sum(jnp.where(col == row + BLOCK, block, 0.0), axis=1, keepdims=True)
        root = lax.rsqrt(pivot)
        root = root * (1.5 - 0.5 * pivot * root * root)
        inverse = (block * root)[:, :BLOCK]
        mine = exact(inverse, work[rows, :], ((1,), (0,)))
        done[rows, :] = mine
        if b < L // BLOCK - 1:
            after = exact(mine[:, :L], mine, ((0,), (0,)))
            work[(b + 1) * BLOCK :, :] -= after[(b + 1) * BLOCK :, :]


def inner_own(p, q):
    dims = (((0,), (0,)), ((), ()))
    (p_h, p_l), (q_h, q_l) = split(p), split(q)

    def pair(u, v):
        return lax.dot_general(u, v, dims, preferred_element_type=F32)

    return pair(p_h, q_h) + (pair(p_h, q_l) + pair(p_l, q_h))


def gram_first(me, link, s, b, reached):
    while reached.count("block") < 1:
        yield
    own = s["own4"][:, :L]
    b["a"][...] = inner_own(own, own).reshape(2, 4, 16, L)
    yield from all_sum(me, link, b)
    gram = b["total"][...].reshape(L, L)
    s["gram"][:L, :L] = gram
    yield from invert_factor(s["work"], s["done0"], gram)
    s["inverse"][:L, :L] = s["done0"][:, L:]
    s["inverse"][:L, L:] = jnp.zeros((L, L), F32)
    reached.append("corner")


def gram_second(me, link, s, b, reached):
    while reached.count("block") < 2:
        yield
    b["a"][...] = inner_own(s["own4"][...], s["own4"][:, L:]).reshape(2, 4, 4, 8, L)
    yield from all_sum(me, link, b)
    while reached.count("corner") < 1:
        yield
    cols = b["total"][...].reshape(256, L)
    cross = cols[:L]
    s["gram"][:, L:] = cols
    s["gram"][L:, :L] = cross.T
    first = s["inverse"][:L, :L]
    upper = exact(first, cross, ((1,), (0,)))
    yield from invert_factor(s["work"], s["done1"], cols[L:] - exact(upper, upper, ((0,), (0,))))
    second = s["done1"][:, L:]
    s["inverse"][L:, L:] = second
    s["inverse"][L:, :L] = -exact(second, exact(upper, first, ((0,), (0,))), ((1,), (0,)))


def projected_task(me, link, s, b, reached):
    while reached.count("image") < 2:
        yield

    def inner(p, q):
        return jnp.dot(p[...], q[...], preferred_element_type=F32)

    part = inner(s["ft_h"], s["img_h"]) + (inner(s["ft_h"], s["img_l"]) + inner(s["ft_l"], s["img_h"]))
    b["a"][...] = part.reshape(2, 4, 4, 8, 256)
    yield from all_sum(me, link, b)


def body_kernel(lap, block, bounds, filtered, rayleigh, *scratch):
    names = [list(group) for group in (SHARED, CHAIN, CHAIN, *REDUCES)]
    groups, at = [], 0
    for group in names:
        groups.append(dict(zip(group, scratch[at : at + len(group)])))
        at += len(group)
    s, chains, reduces = groups[0], groups[1:3], groups[3:]
    lap_sem, *sems = scratch[at:]
    links = [Link(sems[2 * i], sems[2 * i + 1]) for i in range(5)]
    me = Kernel()
    to_row, to_col = me.turn_to()
    alone = jnp.logical_and(to_row == me.r, to_col == me.c)

    load = pltpu.make_async_copy(lap, s["stage"], lap_sem)
    load.start()
    for h, b in enumerate(chains):
        own = b["raw0"].at[me.core, me.x, me.zh]
        own[OWN - 2 :, :] = jnp.zeros((PIECE - OWN + 2, L), F32)
        own[:OWN, :] = block[:, h * L : (h + 1) * L]

    barrier = pltpu.get_barrier_semaphore()
    near = [f(d) for f in (me.yn, me.xn) for d in (1, 2, 3)] + [me.zall(d) for d in range(1, 8)] + [me.cn()]
    for device in near:
        pl.semaphore_signal(barrier, inc=1, device_id=device, device_id_type=MESH)

    @pl.when(jnp.logical_not(alone))
    def _():
        pl.semaphore_signal(barrier, inc=1, device_id=me.turn_to(), device_id_type=MESH)
        pl.semaphore_signal(barrier, inc=1, device_id=me.turn_from(), device_id_type=MESH)

    pl.semaphore_wait(barrier, jnp.where(alone, len(near), len(near) + 2))

    center = (bounds[1] + bounds[0]) * 0.5
    half_width = (bounds[1] - bounds[0]) * 0.5

    def prepare():
        load.wait()
        shift = jnp.where(me.r == me.c, center, 0.0)
        strip = s["strip"]
        strip[...] = jnp.zeros_like(strip)

        def strip_of(start, count):
            value = s["stage"][pl.ds(start, count), :]
            row = start + lax.broadcasted_iota(jnp.int32, (count, TILE), 0)
            col = lax.broadcasted_iota(jnp.int32, (count, TILE), 1)
            strip[:count, :TILE] = value - jnp.where(row == col, shift, 0.0)

        def spread(start):
            whole = strip[...]
            high, low = split(whole)
            s["mat_h"][pl.ds(start, 128), :] = high
            s["mat_l"][pl.ds(start, 128), :] = low
            high, low = split(whole.T)
            s["tra_h"][:, pl.ds(start, 128)] = high
            s["tra_l"][:, pl.ds(start, 128)] = low

        for at in (0, 3, 6, 9):

            @pl.loop(at, min(at + 3, TILE // 128))
            def _(i):
                start = pl.multiple_of(i * 128, 128)
                strip_of(start, 128)
                spread(start)

            yield

        strip[...] = jnp.zeros_like(strip)
        strip_of(TILE // 128 * 128, TILE % 128)
        spread(TILE // 128 * 128)

    s["own4"][PIECE:, :] = jnp.zeros((128 - PIECE, 256), F32)
    reached = []
    one, two = (chain(me, links[h], s, chains[h], h, half_width, alone, reached) for h in (0, 1))
    start = [first_gather(me, links[h], chains[h]) for h in (0, 1)]
    late = together(start[1])
    next(late)
    run(start[0], prepare())

    def second():
        yield from late
        yield from two

    corner = gram_first(me, links[2], s, reduces[0], reached)
    rest = gram_second(me, links[3], s, reduces[1], reached)
    run(one, second(), corner, rest, projected_task(me, links[4], s, reduces[2], reached), rest)
    for c in range(16):

        @pl.when(me.c == c)
        def _(c=c):
            for h, b in enumerate(chains):
                row = 0
                while row < OWN:
                    at = c * OWN + row
                    p, inside = at // PIECE, at % PIECE
                    count = min(PIECE - inside, OWN - row)
                    filtered[row : row + count, h * L : (h + 1) * L] = b["panel_r"][p // 8, (p // 2) % 4, p % 2, inside : inside + count, :]
                    row += count

    projected = reduces[2]["total"][...].reshape(256, 256)
    projected = (projected + projected.T) * 0.5 + center * s["gram"][...]
    inverse = s["inverse"][...]
    rayleigh[...] = exact(exact(inverse, projected, ((1,), (0,))), inverse, ((1,), (1,)))


def body(laplacian, block, bounds):
    vmem = pl.BlockSpec(memory_space=pltpu.VMEM)
    scratch = [pltpu.VMEM(shape, kind) for group in (SHARED, CHAIN, CHAIN, *REDUCES) for shape, kind in group.values()]
    scratch.append(pltpu.SemaphoreType.DMA)
    for count in (CHAIN_SEMS, CHAIN_SEMS, REDUCE_SEMS, REDUCE_SEMS, REDUCE_SEMS):
        scratch += [pltpu.SemaphoreType.DMA((count,)), pltpu.SemaphoreType.DMA((count,))]
    return pl.pallas_call(
        body_kernel,
        out_shape=(jax.ShapeDtypeStruct(block.shape, F32), jax.ShapeDtypeStruct((256, 256), F32)),
        in_specs=[pl.BlockSpec(memory_space=pl.ANY), vmem, pl.BlockSpec(memory_space=pltpu.SMEM)],
        out_specs=(vmem, vmem),
        scratch_shapes=scratch,
        compiler_params=pltpu.CompilerParams(collective_id=0, has_side_effects=True, vmem_limit_bytes=62 * 1024 * 1024),
        name="filter",
    )(laplacian, block, bounds)


def solution(mesh):
    placed = (P("row", "col"), P(("row", "col"), None), P())
    return jax.shard_map(
        body, mesh=mesh, in_specs=placed, out_specs=(P(("row", "col"), None), P()), check_vma=False
    )
```

```python
import jax
import jax.numpy as jnp
from jax import lax
from jax.experimental import pallas as pl
from jax.experimental.pallas import tpu as pltpu
from jax.sharding import PartitionSpec as P

MESH = pl.DeviceIdType.MESH
F32 = jnp.float32
BF16 = jnp.bfloat16
L = 128
TILE = 1440
PAD = 1536
PIECE = 96
OWN = 90

CHAIN = dict(
    raw0=((2, 4, 2, PIECE, L), F32),
    panel0=((PAD, L), F32),
    panel_r=((2, 4, 2, PIECE, L), F32),
    panel_c=((4, 4, 2, 48, L), F32),
    panel_f=((4, 4, 2, 48, L), F32),
    part_c=((4, 4, 2, 48, L), F32),
    part_r=((2, 4, 2, PIECE, L), F32),
    vcat=((PAD, 2 * L), BF16),
    core_in=((4, 2, PIECE, L), F32),
    y_in=((6, 2, 2, 48, L), F32),
    y_sum=((4, 2, 48, L), F32),
    z_in=((3, 2, 48, L), F32),
    x_in=((6, PIECE, L), F32),
    x_sum=((2, PIECE, L), F32),
    h_in=((2, 2, PIECE, L), F32),
    z1=((2, 48, L), F32),
    z2=((2, PIECE, L), F32),
    z4=((2, 48, L), F32),
)
def reduce_of(piece):
    cut = (4, *piece) if piece[0] == 8 else piece
    return dict(
        a=((2, 4, *cut), F32),
        total=((2, 4, *cut), F32),
        core_in=((4, *cut), F32),
        x_in=((3, *cut), F32),
        y_in=((4, *piece), F32),
        z_in=((8, *piece), F32),
    )


REDUCES = reduce_of((16, L)), reduce_of((8, L)), reduce_of((8, 256))
SHARED = dict(
    stage=((TILE, TILE), F32),
    strip=((128, PAD), F32),
    mat_h=((PAD, PAD), BF16),
    mat_l=((PAD, PAD), BF16),
    tra_h=((PAD, PAD), BF16),
    tra_l=((PAD, PAD), BF16),
    own4=((128, 256), F32),
    ft_h=((256, PAD), BF16),
    ft_l=((256, PAD), BF16),
    img_h=((PAD, 256), BF16),
    img_l=((PAD, 256), BF16),
    work=((L, 256), F32),
    done0=((L, 256), F32),
    done1=((L, 256), F32),
    inverse=((256, 256), F32),
    gram=((256, 256), F32),
)
AT_START, AT_ROW, AT_ROWG, AT_COL, AT_COLG, AT_TURN, AT_LAST, CHAIN_SEMS = 0, 11, 20, 29, 39, 49, 50, 59
REDUCE_SEMS = 21


def split(value):
    high = value.astype(BF16)
    return high, (value - high.astype(F32)).astype(BF16)


def together(*tasks):
    tasks = list(tasks)
    while tasks:
        tasks = [t for t in tasks if next(t, "end") != "end"]
        if tasks:
            yield


def run(*tasks):
    for _ in together(*tasks):
        pass


class Kernel:
    def __init__(self):
        r, c = lax.axis_index("row"), lax.axis_index("col")
        self.r, self.c = r, c
        self.y, self.z = r // 4, r % 4
        self.zh, self.x, self.core = c // 8, (c // 2) % 4, c % 2
        self.pos = self.core * 8 + self.x * 2 + self.zh

    def yn(self, d):
        return ((self.y + d) % 4) * 4 + self.z, self.c

    def zn(self, d):
        return self.y * 4 + (self.z + d) % 4, self.c

    def xn(self, d):
        return self.r, self.zh * 8 + ((self.x + d) % 4) * 2 + self.core

    def zall(self, d):
        at = (self.zh * 4 + self.z + d) % 8
        return self.y * 4 + at % 4, (at // 4) * 8 + self.x * 2 + self.core

    def hn(self):
        return self.r, (1 - self.zh) * 8 + self.x * 2 + self.core

    def cn(self):
        return self.r, self.zh * 8 + self.x * 2 + 1 - self.core

    def turn_to(self):
        return self.pos, self.r

    def turn_from(self):
        r = self.r
        return self.c, (r % 2) * 8 + ((r // 2) % 4) * 2 + r // 8


class Link:
    def __init__(self, send, recv):
        self.send, self.recv, self.open = send, recv, []

    def put(self, src, dst, k, device):
        copy = pltpu.make_async_remote_copy(
            src_ref=src, dst_ref=dst, send_sem=self.send.at[k], recv_sem=self.recv.at[k], device_id=device, device_id_type=MESH
        )
        copy.start()
        self.open.append(copy)

    def got(self, dst, k, device):
        pltpu.make_async_remote_copy(
            src_ref=dst, dst_ref=dst, send_sem=self.send.at[k], recv_sem=self.recv.at[k], device_id=device, device_id_type=MESH
        ).wait_recv()

    def flush(self):
        for copy in self.open:
            copy.wait_send()
        self.open = []


def ring_sum(link, k, i, near, half, box, out, ready):
    a, b, d = (i + 1) % 4, (i + 3) % 4, (i + 2) % 4
    ready(d)
    link.put(half(d, 0), box.at[0], k, near(1))
    link.put(half(d, 1), box.at[1], k + 1, near(3))
    ready(a)
    link.put(half(a, 1), box.at[2], k + 2, near(1))
    ready(b)
    link.put(half(b, 0), box.at[3], k + 3, near(3))
    ready(i)
    yield
    link.got(box.at[0], k, near(3))
    half(a, 0)[...] += box[0]
    link.put(half(a, 0), box.at[4], k + 4, near(1))
    link.got(box.at[1], k + 1, near(1))
    half(b, 1)[...] += box[1]
    link.put(half(b, 1), box.at[5], k + 5, near(3))
    yield
    link.got(box.at[2], k + 2, near(3))
    link.got(box.at[3], k + 3, near(1))
    link.got(box.at[4], k + 4, near(3))
    link.got(box.at[5], k + 5, near(1))
    out(0, half(i, 0)[...] + box[4] + box[3])
    out(1, half(i, 1)[...] + box[2] + box[5])


def gather_start(me, link, k, panel):
    own = panel.at[me.core, me.x, me.zh]
    link.put(own, own, k, me.hn())
    yield
    link.got(panel.at[me.core, me.x, 1 - me.zh], k, me.hn())
    yield from gather_col(me, link, k + 1, panel)


def gather_col(me, link, k, panel):
    core, x = me.core, me.x
    a, b, d = (x + 1) % 4, (x + 3) % 4, (x + 2) % 4
    other = 1 - core

    def put(ref, j, device):
        link.put(ref, ref, k + j, device)

    put(panel.at[core, x, 0], 0, me.xn(1))
    put(panel.at[core, x, 1], 1, me.xn(3))
    put(panel.at[core, x, 1], 2, me.xn(1))
    put(panel.at[core, x, 0], 3, me.xn(3))
    put(panel.at[core, x], 6, me.cn())
    yield
    link.got(panel.at[core, b, 0], k, me.xn(3))
    put(panel.at[core, b, 0], 4, me.xn(1))
    link.got(panel.at[core, a, 1], k + 1, me.xn(1))
    put(panel.at[core, a, 1], 5, me.xn(3))
    yield
    link.got(panel.at[core, b, 1], k + 2, me.xn(3))
    put(panel.at[core, b], 7, me.cn())
    link.got(panel.at[core, a, 0], k + 3, me.xn(1))
    put(panel.at[core, a], 8, me.cn())
    link.got(panel.at[core, d, 0], k + 4, me.xn(3))
    link.got(panel.at[core, d, 1], k + 5, me.xn(1))
    put(panel.at[core, d], 9, me.cn())
    yield
    link.got(panel.at[other, x], k + 6, me.cn())
    link.got(panel.at[other, b], k + 7, me.cn())
    link.got(panel.at[other, a], k + 8, me.cn())
    link.got(panel.at[other, d], k + 9, me.cn())


def gather_row(me, link, k, panel):
    y, z = me.y, me.z
    ya, yb, yd = (y + 1) % 4, (y + 3) % 4, (y + 2) % 4

    def put(ref, j, device):
        link.put(ref, ref, k + j, device)

    for d in (1, 2, 3):
        put(panel.at[y, z], d - 1, me.zn(d))
    yield
    for d in (1, 2, 3):
        link.got(panel.at[y, (z + 4 - d) % 4], k + d - 1, me.zn(4 - d))
    low, high = pl.ds(0, 2), pl.ds(2, 2)
    put(panel.at[y, low], 3, me.yn(1))
    put(panel.at[y, high], 4, me.yn(3))
    put(panel.at[y, high], 5, me.yn(1))
    put(panel.at[y, low], 6, me.yn(3))
    yield
    link.got(panel.at[yb, low], k + 3, me.yn(3))
    put(panel.at[yb, low], 7, me.yn(1))
    link.got(panel.at[ya, high], k + 4, me.yn(1))
    put(panel.at[ya, high], 8, me.yn(3))
    yield
    link.got(panel.at[yb, high], k + 5, me.yn(3))
    link.got(panel.at[ya, low], k + 6, me.yn(1))
    link.got(panel.at[yd, low], k + 7, me.yn(3))
    link.got(panel.at[yd, high], k + 8, me.yn(1))


def split_row_panel(panel, vcat):
    @pl.loop(0, 8)
    def _(i):
        high, low = split(panel[i // 4, i % 4].reshape(2 * PIECE, L))
        rows = pl.ds(pl.multiple_of(i * 192, 192), 192)
        vcat[rows, :L] = high
        vcat[rows, L:] = low


def split_col_panel(panel, vcat):
    @pl.loop(0, 4)
    def _(i):
        high, low = split(panel[i].reshape(384, L))
        rows = pl.ds(pl.multiple_of(i * 384, 384), 384)
        vcat[rows, :L] = high
        vcat[rows, L:] = low


def product(high, low, vcat, chunk):
    rows = pl.ds(pl.multiple_of(chunk * 384, 384), 384)
    wide = jnp.dot(high[rows, :], vcat[...], preferred_element_type=F32)
    rest = jnp.dot(low[rows, :], vcat[:, :L], preferred_element_type=F32)
    return wide[:, :L] + (wide[:, L:] + rest)


def odd_step(me, link, s, b, scale, previous, save):
    split_row_panel(b["panel_r"], b["vcat"]) if previous is not None else None
    part, y_sum, panel = b["part_c"], b["y_sum"], b["panel_c"]
    y, z = me.y, me.z

    def ready(j):
        part[j] = product(s["tra_h"], s["tra_l"], b["vcat"], j).reshape(4, 2, 48, L)

    def out_y(h, value):
        y_sum[pl.ds(2 * h, 2)] = value

    yield from ring_sum(link, AT_ROW, y, me.yn, lambda j, h: part.at[j, pl.ds(2 * h, 2)], b["y_in"], out_y, ready)
    box, k = b["z_in"], AT_ROW + 6
    for d in (1, 2, 3):
        link.put(y_sum.at[(z + d) % 4], box.at[d - 1], k + d - 1, me.zn(d))
    yield
    for d in (1, 2, 3):
        link.got(box.at[d - 1], k + d - 1, me.zn(4 - d))
    value = ((y_sum[z] + box[0]) + (box[1] + box[2])) * scale
    if previous is not None:
        value = value - previous[...]
    panel[y, z] = value
    if save is not None:
        save[...] = value
    yield from gather_row(me, link, AT_ROWG, panel)
    link.flush()


def even_sum(me, link, s, b, step, scale, previous, store):
    split_col_panel(b["panel_c"], b["vcat"])
    part, box = b["part_r"], b["core_in"]
    core, x = me.core, me.x
    other, first = 1 - core, 1 - x // 2
    k = AT_COL

    def compute(half, pair):
        value = product(s["mat_h"], s["mat_l"], b["vcat"], half * 2 + pair)
        part[half, pl.ds(2 * pair, 2)] = value.reshape(2, 2, PIECE, L)

    compute(other, first)
    link.put(part.at[other, pl.ds(2 * first, 2)], box.at[pl.ds(2 * first, 2)], k, me.cn())
    last = 1 - first
    compute(other, last)
    link.put(part.at[other, pl.ds(2 * last, 2)], box.at[pl.ds(2 * last, 2)], k + 1, me.cn())
    compute(core, first)
    compute(core, last)
    yield
    turn = []

    def ready(j):
        if len(turn) == 0:
            link.got(box.at[pl.ds(2 * first, 2)], k, me.cn())
        if len(turn) == 1:
            link.got(box.at[pl.ds(2 * last, 2)], k + 1, me.cn())
        turn.append(j)
        part[core, j] += box[j]

    x_sum = b["x_sum"]

    def out_x(h, value):
        x_sum[h] = value

    yield from ring_sum(link, k + 2, x, me.xn, lambda j, h: part.at[core, j, h], b["x_in"], out_x, ready)
    link.put(x_sum, b["h_in"].at[step], k + 8 + step, me.hn())
    yield
    link.got(b["h_in"].at[step], k + 8 + step, me.hn())
    store((x_sum[...] + b["h_in"][step]) * scale - previous())


def first_gather(me, link, b):
    yield from gather_start(me, link, AT_START, b["raw0"])
    panel0 = b["panel0"]
    panel0[TILE:, :] = jnp.zeros((PAD - TILE, L), F32)
    for c in range(16):
        panel0[c * OWN : (c + 1) * OWN, :] = b["raw0"][c % 2, (c // 2) % 4, c // 8, :OWN, :]

    @pl.loop(0, 4)
    def _(i):
        rows = pl.ds(pl.multiple_of(i * 384, 384), 384)
        high, low = split(panel0[rows, :])
        b["vcat"][rows, :L] = high
        b["vcat"][rows, L:] = low

    link.flush()


def chain(me, link, s, b, h, half_width, alone, reached):
    one, two = 1.0 / half_width, 2.0 / half_width
    yield from odd_step(me, link, s, b, one, None, b["z1"])
    panel0, z2, panel_r = b["panel0"], b["z2"], b["panel_r"]

    def store2(value):
        z2[...] = value
        panel_r[me.core, me.x] = value

    rows = pl.ds(pl.multiple_of((me.core * 4 + me.x) * 192, 192), 192)
    yield from even_sum(me, link, s, b, 0, two, lambda: panel0[rows, :].reshape(2, PIECE, L), store2)
    yield from gather_col(me, link, AT_COLG, panel_r)
    link.flush()
    yield from odd_step(me, link, s, b, two, b["z1"], None)

    def store4(value):
        panel_r[me.core, me.x] = value

    yield from even_sum(me, link, s, b, 1, two, lambda: z2[...], store4)
    link.flush()
    b["z4"][...] = panel_r[me.core, me.x, me.zh].reshape(2, 48, L)
    s["own4"][:PIECE, h * L : (h + 1) * L] = b["z4"][...].reshape(PIECE, L)
    reached.append("block")

    def image():
        yield from gather_col(me, link, AT_COLG, panel_r)
        split_row_panel(panel_r, b["vcat"])
        for j in range(4):
            high, low = split(product(s["tra_h"], s["tra_l"], b["vcat"], j))
            s["img_h"][j * 384 : (j + 1) * 384, h * L : (h + 1) * L] = high
            s["img_l"][j * 384 : (j + 1) * 384, h * L : (h + 1) * L] = low

    def rows_across():
        yield from turned_gather(me, link, b, alone)
        for j in range(4):
            high, low = split(b["panel_f"][j].reshape(384, L).T)
            s["ft_h"][h * L : (h + 1) * L, j * 384 : (j + 1) * 384] = high
            s["ft_l"][h * L : (h + 1) * L, j * 384 : (j + 1) * 384] = low

    yield from together(image(), rows_across())
    link.flush()
    reached.append("image")


def turned_gather(me, link, b, alone):
    panel, z4 = b["panel_f"], b["z4"]
    row, col = me.turn_to()
    slot = panel.at[row // 4, row % 4]

    def copy():
        return pltpu.make_async_remote_copy(
            src_ref=z4,
            dst_ref=slot,
            send_sem=link.send.at[AT_TURN],
            recv_sem=link.recv.at[AT_TURN],
            device_id=(row, col),
            device_id_type=MESH,
        )

    @pl.when(jnp.logical_not(alone))
    def _():
        copy().start()

    @pl.when(alone)
    def _():
        panel[me.y, me.z] = z4[...]

    yield

    @pl.when(jnp.logical_not(alone))
    def _():
        link.got(panel.at[me.y, me.z], AT_TURN, me.turn_from())
        copy().wait_send()

    yield from gather_row(me, link, AT_LAST, panel)


def all_sum(me, link, b):
    a, total = b["a"], b["total"]
    y, z, x, core = me.y, me.z, me.x, me.core
    other = 1 - core
    whole = len(a.shape) == 4
    link.put(a.at[other], b["core_in"], 0, me.cn())
    yield
    link.got(b["core_in"], 0, me.cn())
    a[core] += b["core_in"][...]
    for d in (1, 2, 3):
        link.put(a.at[core, (x + d) % 4], b["x_in"].at[d - 1], d, me.xn(d))
    yield
    for d in (1, 2, 3):
        link.got(b["x_in"].at[d - 1], d, me.xn(4 - d))
    near = a[core, x] + ((b["x_in"][0] + b["x_in"][1]) + b["x_in"][2])
    box = b["y_in"]
    if whole:
        box[y] = near
    else:
        a[core, x] = near
        box[y] = a[core, x, y]
    for d in (1, 2, 3):
        place = (y + d) % 4
        link.put(box.at[y] if whole else a.at[core, x, place], box.at[y], 3 + d, me.yn(d))
    yield
    for d in (1, 2, 3):
        link.got(box.at[(y + 4 - d) % 4], 3 + d, me.yn(4 - d))
    at = me.zh * 4 + z
    near, box = (box[0] + box[1]) + (box[2] + box[3]), b["z_in"]
    box[at] = near
    for d in range(1, 8):
        link.put(box.at[at], box.at[at], 6 + d, me.zall(d))
    yield
    for d in range(1, 8):
        link.got(box.at[(at + 8 - d) % 8], 6 + d, me.zall(8 - d))
    near = ((box[0] + box[1]) + (box[2] + box[3])) + ((box[4] + box[5]) + (box[6] + box[7]))
    if whole:
        total[core, x] = near
    else:
        total[core, x, y] = near
        for d in (1, 2, 3):
            link.put(total.at[core, x, y], total.at[core, x, y], 13 + d, me.yn(d))
        yield
        for d in (1, 2, 3):
            link.got(total.at[core, x, (y + 4 - d) % 4], 13 + d, me.yn(4 - d))
    for d in (1, 2, 3):
        link.put(total.at[core, x], total.at[core, x], 16 + d, me.xn(d))
    yield
    for d in (1, 2, 3):
        link.got(total.at[core, (x + 4 - d) % 4], 16 + d, me.xn(4 - d))
    link.put(total.at[core], total.at[core], 20, me.cn())
    yield
    link.got(total.at[other], 20, me.cn())
    link.flush()


BLOCK = 64
GROUPS = BLOCK // 8


def eliminate(groups, turn):
    row = lax.broadcasted_iota(jnp.int32, (8, 128), 0)
    wide = (8, 128)

    def sub(value, j):
        return jnp.broadcast_to(value[j : j + 1, :], wide)

    for j in range(0, 8, 2):
        col0 = [jnp.broadcast_to(g[:, j : j + 1], wide) for g in groups]
        col1 = [jnp.broadcast_to(g[:, j + 1 : j + 2], wide) for g in groups]
        inv0 = 1.0 / sub(col0[0], j)
        lower = sub(col0[0], j + 1) * inv0
        upper = sub(col1[0], j)
        inv1 = 1.0 / (sub(col1[0], j + 1) - lower * upper)
        row0 = sub(groups[0], j)
        row1 = sub(groups[0], j + 1) - lower * row0
        for g in range(GROUPS):
            mul0 = col0[g] * inv0
            mul1 = (col1[g] - mul0 * upper) * inv1
            if g == 0:
                mul0 = jnp.where(row > j, mul0, 0.0)
                mul1 = jnp.where(row > j + 1, mul1, 0.0)
            else:
                left = turn + g < GROUPS
                mul0 = jnp.where(left, mul0, 0.0)
                mul1 = jnp.where(left, mul1, 0.0)
            groups[g] = groups[g] - mul0 * row0 - mul1 * row1
    return [pltpu.roll(g, 120, 1) for g in groups[1:] + groups[:1]]


def exact(p, q, dims):
    return lax.dot_general(p, q, (dims, ((), ())), precision=lax.Precision.HIGHEST, preferred_element_type=F32)


def invert_factor(work, done, gram):
    row = lax.broadcasted_iota(jnp.int32, (L, L), 0)
    col = lax.broadcasted_iota(jnp.int32, (L, L), 1)
    work[:, :L] = gram
    work[:, L:] = jnp.where(row == col, 1.0, 0.0)
    row = lax.broadcasted_iota(jnp.int32, (BLOCK, L), 0)
    col = lax.broadcasted_iota(jnp.int32, (BLOCK, L), 1)
    for b in range(L // BLOCK):
        rows = slice(b * BLOCK, (b + 1) * BLOCK)
        block = work[rows, :L]
        if b % 2:
            block = pltpu.roll(block, 64, 1)
        block = jnp.where(col < BLOCK, block, jnp.where(col == row + BLOCK, 1.0, 0.0))
        groups = tuple(block[8 * g : 8 * g + 8] for g in range(GROUPS))
        for half in range(2):
            at = half * GROUPS // 2
            groups = lax.fori_loop(at, at + GROUPS // 2, lambda i, gs: tuple(eliminate(list(gs), i)), groups)
            yield
        block = jnp.concatenate(groups, axis=0)
        pivot = jnp.sum(jnp.where(col == row + BLOCK, block, 0.0), axis=1, keepdims=True)
        root = lax.rsqrt(pivot)
        root = root * (1.5 - 0.5 * pivot * root * root)
        inverse = (block * root)[:, :BLOCK]
        mine = exact(inverse, work[rows, :], ((1,), (0,)))
        done[rows, :] = mine
        if b < L // BLOCK - 1:
            after = exact(mine[:, :L], mine, ((0,), (0,)))
            work[(b + 1) * BLOCK :, :] -= after[(b + 1) * BLOCK :, :]


def inner_own(p, q):
    dims = (((0,), (0,)), ((), ()))
    (p_h, p_l), (q_h, q_l) = split(p), split(q)

    def pair(u, v):
        return lax.dot_general(u, v, dims, preferred_element_type=F32)

    return pair(p_h, q_h) + (pair(p_h, q_l) + pair(p_l, q_h))


def gram_first(me, link, s, b, reached):
    while reached.count("block") < 1:
        yield
    own = s["own4"][:, :L]
    b["a"][...] = inner_own(own, own).reshape(2, 4, 16, L)
    yield from all_sum(me, link, b)
    gram = b["total"][...].reshape(L, L)
    s["gram"][:L, :L] = gram
    yield from invert_factor(s["work"], s["done0"], gram)
    s["inverse"][:L, :L] = s["done0"][:, L:]
    s["inverse"][:L, L:] = jnp.zeros((L, L), F32)
    reached.append("corner")


def gram_second(me, link, s, b, reached):
    while reached.count("block") < 2:
        yield
    b["a"][...] = inner_own(s["own4"][...], s["own4"][:, L:]).reshape(2, 4, 4, 8, L)
    yield from all_sum(me, link, b)
    while reached.count("corner") < 1:
        yield
    cols = b["total"][...].reshape(256, L)
    cross = cols[:L]
    s["gram"][:, L:] = cols
    s["gram"][L:, :L] = cross.T
    first = s["inverse"][:L, :L]
    upper = exact(first, cross, ((1,), (0,)))
    yield from invert_factor(s["work"], s["done1"], cols[L:] - exact(upper, upper, ((0,), (0,))))
    second = s["done1"][:, L:]
    s["inverse"][L:, L:] = second
    s["inverse"][L:, :L] = -exact(second, exact(upper, first, ((0,), (0,))), ((1,), (0,)))


def projected_task(me, link, s, b, reached):
    while reached.count("image") < 2:
        yield

    def inner(p, q):
        return jnp.dot(p[...], q[...], preferred_element_type=F32)

    part = inner(s["ft_h"], s["img_h"]) + (inner(s["ft_h"], s["img_l"]) + inner(s["ft_l"], s["img_h"]))
    b["a"][...] = part.reshape(2, 4, 4, 8, 256)
    yield from all_sum(me, link, b)


def body_kernel(lap, block, bounds, filtered, rayleigh, *scratch):
    names = [list(group) for group in (SHARED, CHAIN, CHAIN, *REDUCES)]
    groups, at = [], 0
    for group in names:
        groups.append(dict(zip(group, scratch[at : at + len(group)])))
        at += len(group)
    s, chains, reduces = groups[0], groups[1:3], groups[3:]
    lap_sem, *sems = scratch[at:]
    links = [Link(sems[2 * i], sems[2 * i + 1]) for i in range(5)]
    me = Kernel()
    to_row, to_col = me.turn_to()
    alone = jnp.logical_and(to_row == me.r, to_col == me.c)

    load = pltpu.make_async_copy(lap, s["stage"], lap_sem)
    load.start()
    for h, b in enumerate(chains):
        own = b["raw0"].at[me.core, me.x, me.zh]
        own[OWN - 2 :, :] = jnp.zeros((PIECE - OWN + 2, L), F32)
        own[:OWN, :] = block[:, h * L : (h + 1) * L]

    barrier = pltpu.get_barrier_semaphore()
    near = [f(d) for f in (me.yn, me.xn) for d in (1, 2, 3)] + [me.zall(d) for d in range(1, 8)] + [me.cn()]
    for device in near:
        pl.semaphore_signal(barrier, inc=1, device_id=device, device_id_type=MESH)

    pl.semaphore_wait(barrier, len(near))

    center = (bounds[1] + bounds[0]) * 0.5
    half_width = (bounds[1] - bounds[0]) * 0.5

    def prepare():
        load.wait()
        shift = jnp.where(me.r == me.c, center, 0.0)
        strip = s["strip"]
        strip[...] = jnp.zeros_like(strip)

        def strip_of(start, count):
            value = s["stage"][pl.ds(start, count), :]
            row = start + lax.broadcasted_iota(jnp.int32, (count, TILE), 0)
            col = lax.broadcasted_iota(jnp.int32, (count, TILE), 1)
            strip[:count, :TILE] = value - jnp.where(row == col, shift, 0.0)

        def spread(start):
            whole = strip[...]
            high, low = split(whole)
            s["mat_h"][pl.ds(start, 128), :] = high
            s["mat_l"][pl.ds(start, 128), :] = low
            high, low = split(whole.T)
            s["tra_h"][:, pl.ds(start, 128)] = high
            s["tra_l"][:, pl.ds(start, 128)] = low

        for at in (0, 3, 6, 9):

            @pl.loop(at, min(at + 3, TILE // 128))
            def _(i):
                start = pl.multiple_of(i * 128, 128)
                strip_of(start, 128)
                spread(start)

            yield

        strip[...] = jnp.zeros_like(strip)
        strip_of(TILE // 128 * 128, TILE % 128)
        spread(TILE // 128 * 128)

    s["own4"][PIECE:, :] = jnp.zeros((128 - PIECE, 256), F32)
    reached = []
    one, two = (chain(me, links[h], s, chains[h], h, half_width, alone, reached) for h in (0, 1))
    start = [first_gather(me, links[h], chains[h]) for h in (0, 1)]
    late = together(start[1])
    next(late)
    run(start[0], prepare())

    def second():
        yield from late
        yield from two

    corner = gram_first(me, links[2], s, reduces[0], reached)
    rest = gram_second(me, links[3], s, reduces[1], reached)
    run(one, second(), corner, rest, projected_task(me, links[4], s, reduces[2], reached), rest)
    for c in range(16):

        @pl.when(me.c == c)
        def _(c=c):
            for h, b in enumerate(chains):
                row = 0
                while row < OWN:
                    at = c * OWN + row
                    p, inside = at // PIECE, at % PIECE
                    count = min(PIECE - inside, OWN - row)
                    filtered[row : row + count, h * L : (h + 1) * L] = b["panel_r"][p // 8, (p // 2) % 4, p % 2, inside : inside + count, :]
                    row += count

    projected = reduces[2]["total"][...].reshape(256, 256)
    projected = (projected + projected.T) * 0.5 + center * s["gram"][...]
    inverse = s["inverse"][...]
    rayleigh[...] = exact(exact(inverse, projected, ((1,), (0,))), inverse, ((1,), (1,)))


def body(laplacian, block, bounds):
    vmem = pl.BlockSpec(memory_space=pltpu.VMEM)
    scratch = [pltpu.VMEM(shape, kind) for group in (SHARED, CHAIN, CHAIN, *REDUCES) for shape, kind in group.values()]
    scratch.append(pltpu.SemaphoreType.DMA)
    for count in (CHAIN_SEMS, CHAIN_SEMS, REDUCE_SEMS, REDUCE_SEMS, REDUCE_SEMS):
        scratch += [pltpu.SemaphoreType.DMA((count,)), pltpu.SemaphoreType.DMA((count,))]
    return pl.pallas_call(
        body_kernel,
        out_shape=(jax.ShapeDtypeStruct(block.shape, F32), jax.ShapeDtypeStruct((256, 256), F32)),
        in_specs=[pl.BlockSpec(memory_space=pl.ANY), vmem, pl.BlockSpec(memory_space=pltpu.SMEM)],
        out_specs=(vmem, vmem),
        scratch_shapes=scratch,
        compiler_params=pltpu.CompilerParams(collective_id=0, has_side_effects=True, vmem_limit_bytes=62 * 1024 * 1024),
        name="filter",
    )(laplacian, block, bounds)


def solution(mesh):
    placed = (P("row", "col"), P(("row", "col"), None), P())
    return jax.shard_map(
        body, mesh=mesh, in_specs=placed, out_specs=(P(("row", "col"), None), P()), check_vma=False
    )
```
